32 devices in a mesh: vir: 8 (over z, y), fit: 4 (over x, core).
Axes of the slice: x: 2, y: 2, z: 4, core: 2. Of those that a mesh axis runs over, the one named last changes fastest.
Arguments:
- fitted: bfloat16 [2, 2400, 24, 7168], P(None, 'vir', None, 'fit'), may hold values from -0.0234375 to 0.0234375
- vcouple: bfloat16 [2, 2400, 2400], P(None, 'fit'), may hold values from -0.125 to 0.125
- actfock: float32 [2, 24, 24], replicated, may hold values from -1.25 to 1.25
- eps_vir: float32 [2400], P('vir'), may hold values from 0.5 to 4
- eps_act: float32 [24], replicated, may hold values from -0.5 to 0.5
- pair_energy: float32 [64], replicated, may hold values from -3 to -2
- source: float32 [2, 2400, 1536], P(None, 'vir'), may hold values from -6 to 6
Outputs:
- amplitude: float32 [2, 2400, 1536], P(None, 'vir')
The draws below stay inside these ranges and needn't reach their ends.
All inputs are finite; a program needn't handle non-finite values.
Results may differ from the reference program's by a relative error of at most 0.0026.
Values may be sent and summed in bfloat16 or wider, within the bound.
A program may use at most 256 MiB of HBM per device.

```python
import math
import jax
import jax.numpy as jnp
from jax import lax

NACT = 24
NVIR = 2400
NFIT = 7168
PAIRS = 64
PASSES = 3


def steps_of(rng, shape, split, low, top_value):
    factor_of = 1.0
    for position, blocks in split:
        draws = jax.random.uniform(jax.random.fold_in(jax.random.fold_in(rng, 6), position), (blocks,), jnp.float32, low / len(split), top_value / len(split))
        factor_of = factor_of * jnp.repeat(jnp.exp(draws), shape[position] // blocks).reshape((-1,) + (1,) * (len(shape) - 1 - position))
    return factor_of


def scatter_about(rng, shape, scale, bound, shards=(), kind=jnp.bfloat16):
    entries = scale * jax.random.normal(rng, shape, jnp.float32)
    if shards:
        entries = entries * steps_of(rng, shape, shards, -0.22, 0.18)
    return jnp.clip(entries, -bound, bound).astype(kind)


def setup_inputs(seed: int = 0) -> dict:
    arg_keys = jax.random.split(jax.random.key(seed), 8)
    fitted = scatter_about(arg_keys[0], (2, NVIR, NACT, NFIT), (NACT * NVIR) ** -0.5, 0.0234375, ((1, 8), (3, 4)))
    vcouple = scatter_about(arg_keys[1], (2, NVIR, NVIR), NVIR ** -0.5, 0.125, ((1, 4),))
    actfock = scatter_about(arg_keys[2], (2, NACT, NACT), NACT ** -0.5, 1.25, (), jnp.float32)
    eps_vir = jnp.clip(jnp.exp(math.log(4.0) - 2.0794415 * jax.random.uniform(arg_keys[3], (NVIR,), jnp.float32) ** steps_of(arg_keys[3], (NVIR,), ((0, 8),), -0.2, 0.2)), 0.5, 4.0)
    eps_act = jnp.clip(jax.random.uniform(arg_keys[4], (NACT,), jnp.float32, -0.5, 0.5), -0.5, 0.5)
    pair_energy = jnp.clip(jax.random.uniform(arg_keys[5], (PAIRS,), jnp.float32, -3.0, -2.0), -3.0, -2.0)
    source = scatter_about(arg_keys[6], (2, NVIR, NACT * PAIRS), 1.0, 6.0, ((1, 8),), jnp.float32)
    return {"fitted": fitted, "vcouple": vcouple, "actfock": actfock, "eps_vir": eps_vir, "eps_act": eps_act, "pair_energy": pair_energy, "source": source}


def product(left, right):
    return jnp.dot(left, right, precision=lax.Precision.HIGHEST, preferred_element_type=jnp.float32)


def product_first(left, right):
    return lax.dot_general(left, right, (((0,), (0,)), ((), ())), precision=lax.Precision.HIGHEST, preferred_element_type=jnp.float32)


def reference(fitted, vcouple, actfock, eps_vir, eps_act, pair_energy, source):
    highest = lax.Precision.HIGHEST
    denominator = (eps_vir[:, None, None] + eps_act[None, :, None] - pair_energy[None, None, :]).reshape(NVIR, NACT * PAIRS)
    amplitude = source / denominator[None]
    width = NVIR * NACT
    fit_block = NFIT // 8
    fit_real = fitted[0].reshape(width, NFIT)
    fit_imag = fitted[1].reshape(width, NFIT)
    couple_real = vcouple[0].astype(jnp.float32)
    couple_imag = vcouple[1].astype(jnp.float32)
    for pass_index in range(PASSES):
        rounded = amplitude.astype(jnp.bfloat16)
        flat_real = rounded[0].reshape(width, PAIRS).astype(jnp.float32)
        flat_imag = rounded[1].reshape(width, PAIRS).astype(jnp.float32)

        def block(carry, index):
            start = (index * fit_block).astype(jnp.int32)
            piece_real = lax.dynamic_slice_in_dim(fit_real, start, fit_block, 1).astype(jnp.float32)
            piece_imag = lax.dynamic_slice_in_dim(fit_imag, start, fit_block, 1).astype(jnp.float32)
            over_real = product_first(piece_real, flat_real) + product_first(piece_imag, flat_imag)
            over_imag = product_first(piece_real, flat_imag) - product_first(piece_imag, flat_real)
            over_real = lax.optimization_barrier(over_real.astype(jnp.bfloat16)).astype(jnp.float32)
            over_imag = lax.optimization_barrier(over_imag.astype(jnp.bfloat16)).astype(jnp.float32)
            sum_real = carry[0] + product(piece_real, over_real) - product(piece_imag, over_imag)
            sum_imag = carry[1] + product(piece_real, over_imag) + product(piece_imag, over_real)
            return (sum_real, sum_imag), None

        zeros = jnp.zeros((width, PAIRS), jnp.float32)
        sums, ignored = lax.scan(block, (zeros, zeros), jnp.arange(8, dtype=jnp.int32))
        fitted_term = jnp.stack([sums[0], sums[1]]).reshape(2, NVIR, NACT * PAIRS)
        rows_real = rounded[0].astype(jnp.float32)
        rows_imag = rounded[1].astype(jnp.float32)
        vir_real = product_first(couple_real, rows_real) - product_first(couple_imag, rows_imag)
        vir_imag = product_first(couple_imag, rows_real) + product_first(couple_real, rows_imag)
        virtual_term = jnp.stack([vir_real, vir_imag])
        values = amplitude.reshape(2, NVIR, NACT, PAIRS)
        act_real = jnp.einsum("aup,ut->atp", values[0], actfock[0], precision=highest) - jnp.einsum("aup,ut->atp", values[1], actfock[1], precision=highest)
        act_imag = jnp.einsum("aup,ut->atp", values[0], actfock[1], precision=highest) + jnp.einsum("aup,ut->atp", values[1], actfock[0], precision=highest)
        active_term = jnp.stack([act_real, act_imag]).reshape(2, NVIR, NACT * PAIRS)
        residual = source - denominator[None] * amplitude - active_term - fitted_term - virtual_term
        amplitude = amplitude + residual / denominator[None]
    return amplitude
```

```python
import jax
import jax.numpy as jnp
from jax import lax
from jax.experimental import pallas as pl
from jax.experimental.pallas import tpu as pltpu
from jax.sharding import PartitionSpec as P

PASSES = 3
CHUNKS = 3
SLOTS = 3
BF16 = jnp.bfloat16
F32 = jnp.float32
MESH = pl.DeviceIdType.MESH

def contract_first(left, right):
    return lax.dot_general(
        left, right, (((0,), (0,)), ((), ())), preferred_element_type=jnp.float32
    )


def plain_product(left, right):
    return jnp.dot(left, right, preferred_element_type=jnp.float32)


def active_coupling(values, actfock, active, pairs):
    highest = lax.Precision.HIGHEST
    local_vir = values.shape[1]
    grid = values.reshape(2, local_vir, active, pairs)
    act_real = jnp.einsum("aup,ut->atp", grid[0], actfock[0], precision=highest) - jnp.einsum(
        "aup,ut->atp", grid[1], actfock[1], precision=highest
    )
    act_imag = jnp.einsum("aup,ut->atp", grid[0], actfock[1], precision=highest) + jnp.einsum(
        "aup,ut->atp", grid[1], actfock[0], precision=highest
    )
    return jnp.stack([act_real, act_imag]).reshape(2, local_vir, actfock.shape[2] * pairs)


def plain_device(fitted, vcouple, actfock, eps_vir, eps_act, pair_energy, source):
    local_vir = fitted.shape[1]
    active = fitted.shape[2]
    local_fit = fitted.shape[3]
    pairs = pair_energy.shape[0]
    block_rows = vcouple.shape[1]
    width = local_vir * active
    fit_index = lax.axis_index("fit")
    denominator = (
        eps_vir[:, None, None] + eps_act[None, :, None] - pair_energy[None, None, :]
    ).reshape(local_vir, active * pairs)
    amplitude = source / denominator[None]
    fit_real = fitted[0].reshape(width, local_fit)
    fit_imag = fitted[1].reshape(width, local_fit)
    for pass_index in range(PASSES):
        rounded = amplitude.astype(jnp.bfloat16)
        flat_both = jnp.concatenate(
            [rounded[0].reshape(width, pairs), rounded[1].reshape(width, pairs)], axis=1
        )
        real_side = contract_first(fit_real, flat_both)
        imag_side = contract_first(fit_imag, flat_both)
        over_real = real_side[:, :pairs] + imag_side[:, pairs:]
        over_imag = real_side[:, pairs:] - imag_side[:, :pairs]
        intersection = lax.psum(jnp.concatenate([over_real, over_imag], axis=1), "vir").astype(
            jnp.bfloat16
        )
        real_out = plain_product(fit_real, intersection)
        imag_out = plain_product(fit_imag, intersection)
        sum_real = real_out[:, :pairs] - imag_out[:, pairs:]
        sum_imag = real_out[:, pairs:] + imag_out[:, :pairs]
        fitted_part = jnp.stack([sum_real, sum_imag]).reshape(2, local_vir, active * pairs)
        regrouped = lax.all_to_all(rounded, "vir", split_axis=2, concat_axis=1, tiled=True)
        window = lax.dynamic_slice_in_dim(regrouped, fit_index * block_rows, block_rows, 1)
        couple_real = contract_first(vcouple[0], window[0]) - contract_first(vcouple[1], window[1])
        couple_imag = contract_first(vcouple[1], window[0]) + contract_first(vcouple[0], window[1])
        coupled = jnp.stack([couple_real, couple_imag])
        returned = lax.all_to_all(coupled, "vir", split_axis=1, concat_axis=2, tiled=True)
        fitted_part = fitted_part + returned
        total = lax.psum(fitted_part, "fit")
        part_amplitude = amplitude
        active_term = active_coupling(amplitude, actfock, active, pairs)
        residual = source - denominator[None] * part_amplitude - active_term - total
        updated = part_amplitude + residual / denominator[None]
        amplitude = updated
    return amplitude


def turn(values, pairs):
    return jnp.concatenate([-values[..., pairs:], values[..., :pairs]], axis=-1)


def whole_vmem(count):
    return [pl.BlockSpec(memory_space=pltpu.VMEM)] * count


def prologue_kernel(n_fit, eps_ref, row_ref, source_ref, x_ref, src_ref, den_ref, amp_ref, joined, start):
    fit = lax.axis_index("fit")
    local_vir, active, lanes = joined.shape
    pairs = lanes // 2
    for t in range(active):
        cols = slice(t * pairs, (t + 1) * pairs)
        both = jnp.concatenate([source_ref[0, :, cols], source_ref[1, :, cols]], axis=1)
        joined[:, t, :] = both
        start[:, t, :] = both / (eps_ref[...] + row_ref[t : t + 1, :])
    pieces = x_ref.shape[0] * n_fit
    own = local_vir // pieces
    for c in range(x_ref.shape[0]):
        for j in range(n_fit):
            first = (c * n_fit + j) * own
            block = start[first : first + own]
            x_ref[c, j] = block.reshape(own * active, lanes).astype(BF16)
        first = (c * n_fit + fit) * own
        src_ref[c] = joined[pl.ds(first, own)].reshape(own * active, lanes)
        amp_ref[c] = start[pl.ds(first, own)].reshape(own * active, lanes)
        for i in range(own):
            den_ref[c, i * active : (i + 1) * active, :] = eps_ref[first + i] + row_ref[...]


def prologue(eps_vir, row, source, n_fit):
    local_vir = eps_vir.shape[0]
    active, lanes = row.shape
    piece = local_vir // (CHUNKS * n_fit) * active
    own = jax.ShapeDtypeStruct((CHUNKS, piece, lanes), F32)
    return pl.pallas_call(
        lambda *refs: prologue_kernel(n_fit, *refs),
        in_specs=whole_vmem(3),
        out_specs=whole_vmem(4),
        out_shape=[jax.ShapeDtypeStruct((CHUNKS, n_fit, piece, lanes), BF16), own, own, own],
        scratch_shapes=[pltpu.VMEM((local_vir, active, lanes), F32)] * 2,
        compiler_params=pltpu.CompilerParams(vmem_limit_bytes=40 * 2**20),
        name="prologue",
    )(eps_vir[:, None] * jnp.ones((1, lanes), F32), row, source)


def epilogue_kernel(eps_ref, row_ref, source_ref, change_ref, out_ref, wide):
    local_vir, active, lanes = wide.shape
    pairs = lanes // 2
    own = change_ref.shape[1] // active
    for k in range(change_ref.shape[0]):
        wide[k * own : (k + 1) * own] = change_ref[k].astype(F32).reshape(own, active, lanes)
    for t in range(0, active, 2):
        cols = slice(t * pairs, (t + 2) * pairs)
        den = eps_ref[...] + row_ref[:, cols]
        left = wide[:, t, :]
        right = wide[:, t + 1, :]
        real = jnp.concatenate([left[:, :pairs], right[:, :pairs]], axis=1)
        imag = jnp.concatenate([left[:, pairs:], right[:, pairs:]], axis=1)
        out_ref[0, :, cols] = source_ref[0, :, cols] / den + real
        out_ref[1, :, cols] = source_ref[1, :, cols] / den + imag


def epilogue(eps_vir, flat_row, source, change, active, lanes):
    local_vir = eps_vir.shape[0]
    return pl.pallas_call(
        epilogue_kernel,
        in_specs=whole_vmem(4),
        out_specs=pl.BlockSpec(memory_space=pltpu.VMEM),
        out_shape=jax.ShapeDtypeStruct(source.shape, F32),
        scratch_shapes=[pltpu.VMEM((local_vir, active, lanes), F32)],
        compiler_params=pltpu.CompilerParams(vmem_limit_bytes=40 * 2**20),
        name="epilogue",
    )(eps_vir[:, None] * jnp.ones((1, lanes), F32), flat_row, source, change)


def ring_of(vir, n):
    odd = vir % 2
    return (1 - odd) * (vir // 2) + odd * (n - 1 - vir // 2)


def vir_of(pos, n):
    pos = (pos + n) % n
    high = pos // (n // 2)
    return (1 - high) * (2 * pos) + high * (2 * (n - 1 - pos) + 1)


def tile_copy(f_ref, buf, sem, row, tile, slot):
    return pltpu.make_async_copy(f_ref.at[:, pl.ds(row, tile), :], buf.at[slot], sem.at[slot])


def contract_kernel(
    n, f_ref, x_ref, couple_ref, inter_ref, turned_ref, virtual_ref,
    buf, buf_sem, acc, part, parts, whole, ring, spread, rows,
    ring_send, ring_recv, part_send, part_recv, whole_send, whole_recv, own_sem,
):
    vir, fit = lax.axis_index("vir"), lax.axis_index("fit")
    chunks, n_fit, tile, lanes = x_ref.shape
    pairs = lanes // 2
    tiles = chunks * n_fit
    band = lanes // n
    depth = acc.shape[1]
    pos = ring_of(vir, n)
    ahead, behind = vir_of(pos + 1, n), vir_of(pos - 1, n)
    sides = ((ahead, 1), (behind, -1))
    half = n // 2

    def fetch(i, slot):
        return tile_copy(f_ref, buf, buf_sem, pl.multiple_of(i * tile, 8), tile, slot)

    for i in range(SLOTS - 1):
        fetch(i, i).start()

    barrier = pltpu.get_barrier_semaphore()
    for k in range(1, n):
        pl.semaphore_signal(barrier, inc=1, device_id={"vir": (vir + k) % n}, device_id_type=MESH)
    pl.semaphore_wait(barrier, n - 1)

    def hop(side, stage, c, first):
        to, sign = sides[side]
        owner = vir_of(pos - sign * (stage - 1), n)
        return pltpu.make_async_remote_copy(
            src_ref=x_ref.at[c, fit] if first else ring.at[owner, c],
            dst_ref=ring.at[owner, c],
            send_sem=ring_send.at[side, stage - 1, c],
            recv_sem=ring_recv.at[side, stage - 1, c],
            device_id={"vir": to},
            device_id_type=MESH,
        )

    def landed(side, stage, c):
        to, sign = sides[side]
        owner = vir_of(pos - sign * stage, n)
        pltpu.make_async_remote_copy(
            src_ref=ring.at[owner, c],
            dst_ref=ring.at[owner, c],
            send_sem=ring_send.at[side, stage - 1, c],
            recv_sem=ring_recv.at[side, stage - 1, c],
            device_id={"vir": to},
            device_id_type=MESH,
        ).wait_recv()
        return owner

    for c in range(chunks):
        for side in range(2):
            hop(side, 1, c, True).start()
    own_copies = [
        pltpu.make_async_copy(x_ref.at[c, fit], ring.at[vir, c], own_sem.at[c]) for c in range(chunks)
    ]
    for copy in own_copies:
        copy.start()

    active = virtual_ref.shape[1]
    own = tile // active
    span = spread.shape[0] // active
    spread[...] = jnp.zeros_like(spread)

    def lay(owner, c):
        spread[0:tile, :] = ring[owner, c].astype(F32)
        top = pl.multiple_of((c * n + owner) * span, span)
        for t in range(active):
            rows[pl.ds(top, span), t * lanes : (t + 1) * lanes] = spread[
                pl.ds(t, span, stride=active), :
            ].astype(BF16)

    last = [(half, c) for c in range(chunks)]
    split = (chunks + 1) // 2

    def sent_last(side, c):
        return (c < split) if side == 0 else (c >= split)

    def relay(stage, c):
        for side in range(2):
            owner = landed(side, stage, c)

            @pl.when((stage < half - 1) | sent_last(side, c))
            def _():
                hop(side, stage + 1, c, False).start()

            lay(owner, c)

    relays = chunks * (half - 1)
    acc[...] = jnp.zeros_like(acc)
    contract = (((0,), (0,)), ((), ()))

    def step(i, carry):
        @pl.when(i + SLOTS - 1 < tiles)
        def _():
            fetch(i + SLOTS - 1, lax.rem(i + SLOTS - 1, SLOTS)).start()

        slot = lax.rem(i, SLOTS)
        fetch(i, slot).wait()
        values = x_ref[i // n_fit, lax.rem(i, n_fit)]
        acc[...] += lax.dot_general(
            values, buf[slot, 0], contract, preferred_element_type=F32
        ) + lax.dot_general(-turn(values, pairs), buf[slot, 1], contract, preferred_element_type=F32)

        @pl.when((lax.rem(i, 2) == 1) & (i // 2 < relays))
        def _():
            r = i // 2
            relay(1 + r // chunks, lax.rem(r, chunks))

        return carry

    lax.fori_loop(0, tiles, step, 0)

    def part_copy(k):
        peer = (vir + k) % n
        return pltpu.make_async_remote_copy(
            src_ref=part.at[peer],
            dst_ref=parts.at[vir],
            send_sem=part_send.at[k - 1],
            recv_sem=part_recv.at[k - 1],
            device_id={"vir": peer},
            device_id_type=MESH,
        )

    def part_landed(k):
        peer = (vir + n - k) % n
        pltpu.make_async_remote_copy(
            src_ref=part.at[peer],
            dst_ref=parts.at[peer],
            send_sem=part_send.at[k - 1],
            recv_sem=part_recv.at[k - 1],
            device_id={"vir": peer},
            device_id_type=MESH,
        ).wait_recv()

    for k in range(n):
        part[k] = acc[k * band : (k + 1) * band, :].astype(BF16)
    for k in range(1, n):
        part_copy(k).start()
    done = min(tiles // 2, relays)

    def more(r, carry):
        relay(1 + r // chunks, lax.rem(r, chunks))
        return carry

    if relays > done:
        lax.fori_loop(done, done + 1, more, 0)
    total = acc[pl.ds(pl.multiple_of(vir * band, band), band), :]
    for k in range(1, n):
        part_landed(k)
        total = total + parts[(vir + n - k) % n].astype(F32)
    whole[vir] = total.astype(BF16)

    def whole_copy(k):
        peer = (vir + k) % n
        return pltpu.make_async_remote_copy(
            src_ref=whole.at[vir],
            dst_ref=whole.at[vir],
            send_sem=whole_send.at[k - 1],
            recv_sem=whole_recv.at[k - 1],
            device_id={"vir": peer},
            device_id_type=MESH,
        )

    def whole_landed(k):
        peer = (vir + n - k) % n
        pltpu.make_async_remote_copy(
            src_ref=whole.at[peer],
            dst_ref=whole.at[peer],
            send_sem=whole_send.at[k - 1],
            recv_sem=whole_recv.at[k - 1],
            device_id={"vir": peer},
            device_id_type=MESH,
        ).wait_recv()

    for k in range(1, n):
        whole_copy(k).start()
    if relays > done + 1:
        lax.fori_loop(done + 1, relays, more, 0)
    for c in range(chunks):
        own_copies[c].wait()
        lay(vir, c)
    for c in range(chunks):
        side = 0 if c < split else 1
        lay(landed(side, half, c), c)
    for k in range(1, n):
        whole_landed(k)
    block = depth
    for width in (512, 384, 256, 128):
        if depth % width == 0:
            block = width
            break
    for q in range(0, depth, block):
        cols = whole[:, :, q : q + block].reshape(lanes, block).astype(F32).T
        inter_ref[q : q + block, :] = cols.astype(BF16)
        turned_ref[q : q + block, :] = turn(cols, pairs).astype(BF16)
    for t in range(0, active, 2):
        left = rows[:, t * lanes : (t + 1) * lanes]
        right = rows[:, (t + 1) * lanes : (t + 2) * lanes]
        plain = jnp.concatenate([left, right], axis=1)
        other = jnp.concatenate([turn(left, pairs), turn(right, pairs)], axis=1)
        value = plain_product(couple_ref[0], plain) + plain_product(couple_ref[1], other)
        virtual_ref[:, t, :] = value[:, :lanes]
        virtual_ref[:, t + 1, :] = value[:, lanes:]

    for c in range(chunks):
        for side in range(2):
            for stage in range(1, half + 1):
                if stage < half or sent_last(side, c):
                    hop(side, stage, c, stage == 1).wait_send()
    for k in range(1, n):
        part_copy(k).wait_send()
        whole_copy(k).wait_send()


def contraction(fit_rows, values, couple, active, n):
    depth = fit_rows.shape[2]
    chunks, n_fit, tile, lanes = values.shape
    local_vir, wide = couple.shape[1:]
    span = wide // (chunks * n)
    half = n // 2
    dma = pltpu.SemaphoreType.DMA
    return pl.pallas_call(
        lambda *refs: contract_kernel(n, *refs),
        in_specs=[pl.BlockSpec(memory_space=pl.ANY)] + whole_vmem(2),
        out_specs=whole_vmem(3),
        out_shape=[
            jax.ShapeDtypeStruct((depth, lanes), BF16),
            jax.ShapeDtypeStruct((depth, lanes), BF16),
            jax.ShapeDtypeStruct((local_vir, active, lanes), F32),
        ],
        scratch_shapes=[
            pltpu.VMEM((SLOTS, 2, tile, depth), BF16),
            dma((SLOTS,)),
            pltpu.VMEM((lanes, depth), F32),
            pltpu.VMEM((n, lanes // n, depth), BF16),
            pltpu.VMEM((n, lanes // n, depth), BF16),
            pltpu.VMEM((n, lanes // n, depth), BF16),
            pltpu.VMEM((n, chunks, tile, lanes), BF16),
            pltpu.VMEM((span * active, lanes), F32),
            pltpu.VMEM((wide, active * lanes), BF16),
            dma((2, half, chunks)),
            dma((2, half, chunks)),
            dma((n - 1,)),
            dma((n - 1,)),
            dma((n - 1,)),
            dma((n - 1,)),
            dma((chunks,)),
        ],
        compiler_params=pltpu.CompilerParams(
            collective_id=0, has_side_effects=True, vmem_limit_bytes=56 * 2**20
        ),
        name="contraction",
    )(fit_rows, values, couple)


def back_kernel(
    final, f_ref, inter_ref, turned_ref, virtual_ref, src_ref, den_ref, amp_ref, act_ref,
    x_ref, new_ref,
    buf, buf_sem, near, near_in, far, far_in, kept,
    near_send, near_recv, far_send, far_recv, gx_send, gx_recv, gc_send, gc_recv, gr_send, gr_recv,
):
    fit = lax.axis_index("fit")
    x, core = fit // 2, fit % 2
    chunks, n_fit, tile, lanes = x_ref.shape
    pairs = lanes // 2
    tiles = chunks * n_fit
    beside = x * 2 + (1 - core)
    across = (1 - x) * 2 + core
    order = ((1 - x) * 2 + (1 - core), beside, across, fit)

    def where(i):
        k = i % n_fit
        return (i - k) + order[k]

    def fetch(i):
        row = pl.multiple_of(where(i) * tile, 8)
        return tile_copy(f_ref, buf, buf_sem, row, tile, i % SLOTS)

    for i in range(SLOTS - 1):
        fetch(i).start()

    barrier = pltpu.get_barrier_semaphore()
    for peer in (beside, across):
        pl.semaphore_signal(barrier, inc=1, device_id={"fit": peer}, device_id_type=MESH)
    pl.semaphore_wait(barrier, 2)

    def copy(src, dst, send, recv, peer):
        return pltpu.make_async_remote_copy(
            src_ref=src, dst_ref=dst, send_sem=send, recv_sem=recv,
            device_id={"fit": peer}, device_id_type=MESH,
        )

    def near_copy(c, k):
        return copy(near.at[c, k], near_in.at[c, k], near_send.at[c, k], near_recv.at[c, k], beside)

    def far_copy(c):
        return copy(far.at[c], far_in.at[c], far_send.at[c], far_recv.at[c], across)

    def gather_across(c, owner):
        return copy(x_ref.at[c, owner], x_ref.at[c, owner], gx_send.at[c], gx_recv.at[c], across)

    def gather_beside(c, owner):
        return copy(x_ref.at[c, owner], x_ref.at[c, owner], gc_send.at[c], gc_recv.at[c], beside)

    def gather_relay(c, owner):
        return copy(x_ref.at[c, owner], x_ref.at[c, owner], gr_send.at[c], gr_recv.at[c], beside)

    group = act_ref.shape[1]

    def update(c):
        far_copy(c).wait_recv()
        for g in range(0, tile, group):
            part = slice(g, g + group)
            value = amp_ref[c, part, :]
            act = jnp.dot(
                act_ref[0], value, precision=lax.Precision.HIGHEST, preferred_element_type=F32
            ) + jnp.dot(
                act_ref[1], turn(value, pairs), precision=lax.Precision.HIGHEST,
                preferred_element_type=F32,
            )
            total = kept[c, part, :] + far_in[c, part, :].astype(F32)
            den = den_ref[c, part, :]
            fresh = (src_ref[c, part, :] - act - total) / den
            new_ref[c, part, :] = fresh
            if final:
                kept[c, part, :] = fresh - src_ref[c, part, :] / den
            else:
                kept[c, part, :] = fresh
        x_ref[c, fit] = kept[c].astype(BF16)
        gather_across(c, fit).start()
        gather_beside(c, fit).start()

    def pass_on(c):
        gather_across(c, across).wait_recv()
        gather_relay(c, across).start()

    for i in range(tiles):
        if i + SLOTS - 1 < tiles:
            fetch(i + SLOTS - 1).start()
        c, k = divmod(i, n_fit)
        fetch(i).wait()
        slot = i % SLOTS
        value = (
            plain_product(buf[slot, 0], inter_ref[...])
            + plain_product(buf[slot, 1], turned_ref[...])
            + virtual_ref[where(i)]
        )
        if k < 2:
            near[c, k] = value.astype(BF16)
            near_copy(c, k).start()
        elif k == 2:
            near_copy(c, 0).wait_recv()
            far[c] = (value + near_in[c, 0].astype(F32)).astype(BF16)
            far_copy(c).start()
        else:
            near_copy(c, 1).wait_recv()
            kept[c] = value + near_in[c, 1].astype(F32)
        if k == 1 and c >= 1:
            update(c - 1)
        if k == 1 and c >= 2:
            pass_on(c - 2)
    if chunks >= 2:
        pass_on(chunks - 2)
    update(chunks - 1)
    pass_on(chunks - 1)
    for c in range(chunks):
        gather_beside(c, beside).wait_recv()
        gather_relay(c, order[0]).wait_recv()
    for c in range(chunks):
        for k in range(2):
            near_copy(c, k).wait_send()
        far_copy(c).wait_send()
        gather_across(c, fit).wait_send()
        gather_beside(c, fit).wait_send()
        gather_relay(c, across).wait_send()


def back(fit_rows, inter, turned, virtual, src, den, amp, act, n_fit, final):
    depth = fit_rows.shape[2]
    chunks, tile, lanes = src.shape
    dma = pltpu.SemaphoreType.DMA
    each = pltpu.VMEM((chunks, tile, lanes), BF16)
    twice = pltpu.VMEM((chunks, 2, tile, lanes), BF16)
    virtual = virtual.reshape(chunks * n_fit, tile, lanes)
    return pl.pallas_call(
        lambda *refs: back_kernel(final, *refs),
        in_specs=[pl.BlockSpec(memory_space=pl.ANY)] + whole_vmem(7),
        out_specs=whole_vmem(2),
        out_shape=[
            jax.ShapeDtypeStruct((chunks, n_fit, tile, lanes), BF16),
            jax.ShapeDtypeStruct((chunks, tile, lanes), F32),
        ],
        scratch_shapes=[
            pltpu.VMEM((SLOTS, 2, tile, depth), BF16),
            dma((SLOTS,)),
            twice,
            twice,
            each,
            each,
            pltpu.VMEM((chunks, tile, lanes), F32),
        ]
        + [dma((chunks, 2))] * 2
        + [dma((chunks,))] * 8,
        compiler_params=pltpu.CompilerParams(
            collective_id=2 if final else 1, has_side_effects=True, vmem_limit_bytes=56 * 2**20
        ),
        name="back",
    )(fit_rows, inter, turned, virtual, src, den, amp, act)


def per_device(fitted, vcouple, actfock, eps_vir, eps_act, pair_energy, source):
    n_fit, n_vir = lax.axis_size("fit"), lax.axis_size("vir")
    vir_index = lax.axis_index("vir")
    local_vir, active, local_fit = fitted.shape[1:]
    block_rows = vcouple.shape[1]
    pairs = pair_energy.shape[0]
    lanes = 2 * pairs
    own = local_vir // (CHUNKS * n_fit)
    span = -(-own // 16) * 16
    held = block_rows // local_vir

    row = eps_act[:, None] - pair_energy[None, :]
    wide_row = jnp.concatenate([row, row], axis=1)
    values, src, den, amp = prologue(eps_vir, wide_row, source, n_fit)

    couple = lax.dynamic_slice_in_dim(vcouple, vir_index * local_vir, local_vir, 2)
    couple = couple.reshape(2, held, CHUNKS, n_fit, own, local_vir).transpose(3, 0, 1, 2, 4, 5)
    couple = couple.reshape(n_fit, 2 * held * CHUNKS * own, local_vir)
    couple = lax.all_to_all(couple, "fit", 0, 0)
    couple = couple.reshape(n_fit, 2, held, CHUNKS, own, local_vir).transpose(1, 5, 3, 0, 2, 4)
    couple = jnp.pad(couple, ((0, 0),) * 5 + ((0, span - own),))
    couple = couple.reshape(2, local_vir, CHUNKS * n_vir * span)

    group = 5
    eye = jnp.eye(group, dtype=F32)
    act = jnp.einsum("gh,cut->cgthu", eye, actfock).reshape(2, group * active, group * active)
    fit_rows = fitted.reshape(2, local_vir * active, local_fit)
    for pass_index in range(PASSES):
        inter, turned, virtual = contraction(fit_rows, values, couple, active, n_vir)
        values, amp = back(
            fit_rows, inter, turned, virtual, src, den, amp, act, n_fit, pass_index == PASSES - 1
        )
    change = values.reshape(CHUNKS * n_fit, own * active, lanes)
    return epilogue(eps_vir, row.reshape(1, active * pairs), source, change, active, lanes)


def choose(mesh):
    def body(*args):
        n_fit, n_vir = mesh.shape["fit"], mesh.shape["vir"]
        fitted, vcouple, actfock, eps_vir, eps_act, pair_energy, source = args
        local_vir, active, local_fit = fitted.shape[1:]
        fits = (
            n_fit == 4
            and n_vir % 2 == 0
            and 2 * pair_energy.shape[0] == 128
            and n_vir * 16 == 128
            and local_vir % (CHUNKS * n_fit * 5) == 0
            and vcouple.shape[1] % local_vir == 0
            and active % 8 == 0
            and local_fit % 128 == 0
        )
        return per_device(*args) if fits else plain_device(*args)

    return body


def solution(mesh):
    return jax.shard_map(
        choose(mesh),
        mesh=mesh,
        in_specs=(
            P(None, "vir", None, "fit"),
            P(None, "fit", None),
            P(),
            P("vir"),
            P(),
            P(),
            P(None, "vir", None),
        ),
        out_specs=P(None, "vir", None),
        check_vma=False,
    )
```

```python
import jax
import jax.numpy as jnp
from jax import lax
from jax.experimental import pallas as pl
from jax.experimental.pallas import tpu as pltpu
from jax.sharding import PartitionSpec as P

PASSES = 3
CHUNKS = 3
SLOTS = 3
BF16 = jnp.bfloat16
F32 = jnp.float32
MESH = pl.DeviceIdType.MESH

def contract_first(left, right):
    return lax.dot_general(
        left, right, (((0,), (0,)), ((), ())), preferred_element_type=jnp.float32
    )


def plain_product(left, right):
    return jnp.dot(left, right, preferred_element_type=jnp.float32)


def active_coupling(values, actfock, active, pairs):
    highest = lax.Precision.HIGHEST
    local_vir = values.shape[1]
    grid = values.reshape(2, local_vir, active, pairs)
    act_real = jnp.einsum("aup,ut->atp", grid[0], actfock[0], precision=highest) - jnp.einsum(
        "aup,ut->atp", grid[1], actfock[1], precision=highest
    )
    act_imag = jnp.einsum("aup,ut->atp", grid[0], actfock[1], precision=highest) + jnp.einsum(
        "aup,ut->atp", grid[1], actfock[0], precision=highest
    )
    return jnp.stack([act_real, act_imag]).reshape(2, local_vir, actfock.shape[2] * pairs)


def plain_device(fitted, vcouple, actfock, eps_vir, eps_act, pair_energy, source):
    local_vir = fitted.shape[1]
    active = fitted.shape[2]
    local_fit = fitted.shape[3]
    pairs = pair_energy.shape[0]
    block_rows = vcouple.shape[1]
    width = local_vir * active
    fit_index = lax.axis_index("fit")
    denominator = (
        eps_vir[:, None, None] + eps_act[None, :, None] - pair_energy[None, None, :]
    ).reshape(local_vir, active * pairs)
    amplitude = source / denominator[None]
    fit_real = fitted[0].reshape(width, local_fit)
    fit_imag = fitted[1].reshape(width, local_fit)
    for pass_index in range(PASSES):
        rounded = amplitude.astype(jnp.bfloat16)
        flat_both = jnp.concatenate(
            [rounded[0].reshape(width, pairs), rounded[1].reshape(width, pairs)], axis=1
        )
        real_side = contract_first(fit_real, flat_both)
        imag_side = contract_first(fit_imag, flat_both)
        over_real = real_side[:, :pairs] + imag_side[:, pairs:]
        over_imag = real_side[:, pairs:] - imag_side[:, :pairs]
        intersection = lax.psum(jnp.concatenate([over_real, over_imag], axis=1), "vir").astype(
            jnp.bfloat16
        )
        real_out = plain_product(fit_real, intersection)
        imag_out = plain_product(fit_imag, intersection)
        sum_real = real_out[:, :pairs] - imag_out[:, pairs:]
        sum_imag = real_out[:, pairs:] + imag_out[:, :pairs]
        fitted_part = jnp.stack([sum_real, sum_imag]).reshape(2, local_vir, active * pairs)
        regrouped = lax.all_to_all(rounded, "vir", split_axis=2, concat_axis=1, tiled=True)
        window = lax.dynamic_slice_in_dim(regrouped, fit_index * block_rows, block_rows, 1)
        couple_real = contract_first(vcouple[0], window[0]) - contract_first(vcouple[1], window[1])
        couple_imag = contract_first(vcouple[1], window[0]) + contract_first(vcouple[0], window[1])
        coupled = jnp.stack([couple_real, couple_imag])
        returned = lax.all_to_all(coupled, "vir", split_axis=1, concat_axis=2, tiled=True)
        fitted_part = fitted_part + returned
        total = lax.psum(fitted_part, "fit")
        part_amplitude = amplitude
        active_term = active_coupling(amplitude, actfock, active, pairs)
        residual = source - denominator[None] * part_amplitude - active_term - total
        updated = part_amplitude + residual / denominator[None]
        amplitude = updated
    return amplitude


def turn(values, pairs):
    return jnp.concatenate([-values[..., pairs:], values[..., :pairs]], axis=-1)


def whole_vmem(count):
    return [pl.BlockSpec(memory_space=pltpu.VMEM)] * count


def prologue_kernel(n_fit, eps_ref, row_ref, source_ref, x_ref, src_ref, den_ref, joined, start):
    fit = lax.axis_index("fit")
    local_vir, active, lanes = joined.shape
    pairs = lanes // 2
    for t in range(active):
        cols = slice(t * pairs, (t + 1) * pairs)
        both = jnp.concatenate([source_ref[0, :, cols], source_ref[1, :, cols]], axis=1)
        joined[:, t, :] = both
        start[:, t, :] = both / (eps_ref[...] + row_ref[t : t + 1, :])
    pieces = x_ref.shape[0] * n_fit
    own = local_vir // pieces
    for c in range(x_ref.shape[0]):
        for j in range(n_fit):
            first = (c * n_fit + j) * own
            block = start[first : first + own]
            x_ref[c, j] = block.reshape(own * active, lanes).astype(BF16)
        first = (c * n_fit + fit) * own
        src_ref[c] = joined[pl.ds(first, own)].reshape(own * active, lanes)
        for i in range(own):
            den_ref[c, i * active : (i + 1) * active, :] = eps_ref[first + i] + row_ref[...]


def prologue(eps_vir, row, source, n_fit):
    local_vir = eps_vir.shape[0]
    active, lanes = row.shape
    piece = local_vir // (CHUNKS * n_fit) * active
    own = jax.ShapeDtypeStruct((CHUNKS, piece, lanes), F32)
    return pl.pallas_call(
        lambda *refs: prologue_kernel(n_fit, *refs),
        in_specs=whole_vmem(3),
        out_specs=whole_vmem(3),
        out_shape=[jax.ShapeDtypeStruct((CHUNKS, n_fit, piece, lanes), BF16), own, own],
        scratch_shapes=[pltpu.VMEM((local_vir, active, lanes), F32)] * 2,
        compiler_params=pltpu.CompilerParams(vmem_limit_bytes=40 * 2**20),
        name="prologue",
    )(eps_vir[:, None] * jnp.ones((1, lanes), F32), row, source)


def epilogue_kernel(eps_ref, row_ref, source_ref, change_ref, out_ref, wide):
    local_vir, active, lanes = wide.shape
    pairs = lanes // 2
    own = change_ref.shape[1] // active
    for k in range(change_ref.shape[0]):
        wide[k * own : (k + 1) * own] = change_ref[k].astype(F32).reshape(own, active, lanes)
    for t in range(0, active, 2):
        cols = slice(t * pairs, (t + 2) * pairs)
        den = eps_ref[...] + row_ref[:, cols]
        left = wide[:, t, :]
        right = wide[:, t + 1, :]
        real = jnp.concatenate([left[:, :pairs], right[:, :pairs]], axis=1)
        imag = jnp.concatenate([left[:, pairs:], right[:, pairs:]], axis=1)
        out_ref[0, :, cols] = source_ref[0, :, cols] / den + real
        out_ref[1, :, cols] = source_ref[1, :, cols] / den + imag


def epilogue(eps_vir, flat_row, source, change, active, lanes):
    local_vir = eps_vir.shape[0]
    return pl.pallas_call(
        epilogue_kernel,
        in_specs=whole_vmem(4),
        out_specs=pl.BlockSpec(memory_space=pltpu.VMEM),
        out_shape=jax.ShapeDtypeStruct(source.shape, F32),
        scratch_shapes=[pltpu.VMEM((local_vir, active, lanes), F32)],
        compiler_params=pltpu.CompilerParams(vmem_limit_bytes=40 * 2**20),
        name="epilogue",
    )(eps_vir[:, None] * jnp.ones((1, lanes), F32), flat_row, source, change)


def ring_of(vir, n):
    odd = vir % 2
    return (1 - odd) * (vir // 2) + odd * (n - 1 - vir // 2)


def vir_of(pos, n):
    pos = (pos + n) % n
    high = pos // (n // 2)
    return (1 - high) * (2 * pos) + high * (2 * (n - 1 - pos) + 1)


def choose_int(index, table):
    value = 0
    for key, entry in table.items():
        value = value + jnp.where(index == key, entry, 0)
    return value


def passes_kernel(
    n, f_ref, start_ref, couple_ref, src_ref, den_ref, act_ref, x_ref,
    buf, buf_sem, acc, part, parts, whole, inter, turned, ring, spread, rows, virtual,
    near, near_in, far, far_in, kept, amp,
    ring_send, ring_recv, part_send, part_recv, whole_send, whole_recv, init_sem,
    near_send, near_recv, far_send, far_recv, gx_send, gx_recv, gc_send, gc_recv, gr_send, gr_recv,
):
    vir, fit = lax.axis_index("vir"), lax.axis_index("fit")
    chunks, n_fit, tile, lanes = x_ref.shape
    pairs = lanes // 2
    tiles = chunks * n_fit
    band = lanes // n
    depth = acc.shape[1]
    active = virtual.shape[1]
    span = spread.shape[0] // active
    half = n // 2
    pos = ring_of(vir, n)
    sides = ((vir_of(pos + 1, n), 1), (vir_of(pos - 1, n), -1))
    x, core = fit // 2, fit % 2
    beside = x * 2 + (1 - core)
    across = (1 - x) * 2 + core
    order = ((1 - x) * 2 + (1 - core), beside, across, fit)
    split = (chunks + 1) // 2
    group = act_ref.shape[1]

    def fetch(row_tile, slot):
        row = pl.multiple_of(row_tile * tile, 8)
        return pltpu.make_async_copy(
            f_ref.at[:, pl.ds(row, tile), :], buf.at[slot], buf_sem.at[slot]
        )

    def remote(src, dst, send, recv, axis, peer):
        return pltpu.make_async_remote_copy(
            src_ref=src, dst_ref=dst, send_sem=send, recv_sem=recv,
            device_id={axis: peer}, device_id_type=MESH,
        )

    def back_tile(k):
        value = 0
        for j in range(n_fit):
            value = value + jnp.where(k == j, order[j], 0)
        return value

    for i in range(SLOTS - 1):
        fetch(i, i).start()
    inits = [
        pltpu.make_async_copy(start_ref.at[c], x_ref.at[c], init_sem.at[0, c]) for c in range(chunks)
    ] + [
        pltpu.make_async_copy(start_ref.at[c, fit], ring.at[0, vir, c], init_sem.at[1, c])
        for c in range(chunks)
    ]
    for init in inits:
        init.start()

    barrier = pltpu.get_barrier_semaphore()
    for k in range(1, n):
        pl.semaphore_signal(barrier, inc=1, device_id={"vir": (vir + k) % n}, device_id_type=MESH)
    for peer in (beside, across):
        pl.semaphore_signal(barrier, inc=1, device_id={"fit": peer}, device_id_type=MESH)

    for c in range(chunks):
        amp[c] = src_ref[c] / den_ref[c]
    spread[...] = jnp.zeros_like(spread)
    for init in inits:
        init.wait()
    pl.semaphore_wait(barrier, n + 1)

    def sent_last(side, c):
        return (c < split) if side == 0 else (c >= split)

    def hop(parity, side, stage, c):
        to, sign = sides[side]
        owner = vir_of(pos - sign * (stage - 1), n)
        slot = ring.at[parity, owner, c]
        return remote(
            slot, slot, ring_send.at[side, stage - 1, c], ring_recv.at[side, stage - 1, c], "vir", to
        )

    def lay(parity, owner, c):
        spread[0:tile, :] = ring[parity, owner, c].astype(F32)
        top = pl.multiple_of((c * n + owner) * span, span)
        for t in range(active):
            rows[pl.ds(top, span), t * lanes : (t + 1) * lanes] = spread[
                pl.ds(t, span, stride=active), :
            ].astype(BF16)

    def landed(parity, side, stage, c):
        to, sign = sides[side]
        owner = vir_of(pos - sign * stage, n)
        slot = ring.at[parity, owner, c]
        remote(
            slot, slot, ring_send.at[side, stage - 1, c], ring_recv.at[side, stage - 1, c], "vir", to
        ).wait_recv()
        return owner

    def open_ring(parity, c):
        for side in range(2):
            hop(parity, side, 1, c).start()

    def relay(parity, stage, c):
        owners = []
        for side in range(2):
            owners.append(landed(parity, side, stage, c))

            @pl.when((stage < half - 1) | sent_last(side, c))
            def _():
                hop(parity, side, stage + 1, c).start()

        for owner in owners:
            lay(parity, owner, c)

    def part_copy(k):
        peer = (vir + k) % n
        return remote(
            part.at[peer], parts.at[vir], part_send.at[k - 1], part_recv.at[k - 1], "vir", peer
        )

    def part_landed(k):
        peer = (vir + n - k) % n
        remote(
            part.at[peer], parts.at[peer], part_send.at[k - 1], part_recv.at[k - 1], "vir", peer
        ).wait_recv()
        return peer

    def whole_copy(k):
        peer = (vir + k) % n
        return remote(
            whole.at[vir], whole.at[vir], whole_send.at[k - 1], whole_recv.at[k - 1], "vir", peer
        )

    def whole_landed(k):
        peer = (vir + n - k) % n
        remote(
            whole.at[peer], whole.at[peer], whole_send.at[k - 1], whole_recv.at[k - 1], "vir", peer
        ).wait_recv()

    def near_copy(c, k):
        return remote(
            near.at[c, k], near_in.at[c, k], near_send.at[c, k], near_recv.at[c, k], "fit", beside
        )

    def far_copy(c):
        return remote(far.at[c], far_in.at[c], far_send.at[c], far_recv.at[c], "fit", across)

    def gather_across(c, owner):
        slot = x_ref.at[c, owner]
        return remote(slot, slot, gx_send.at[c], gx_recv.at[c], "fit", across)

    def gather_beside(c, owner):
        slot = x_ref.at[c, owner]
        return remote(slot, slot, gc_send.at[c], gc_recv.at[c], "fit", beside)

    def gather_relay(c, owner):
        slot = x_ref.at[c, owner]
        return remote(slot, slot, gr_send.at[c], gr_recv.at[c], "fit", beside)

    def update(c, parity, final):
        far_copy(c).wait_recv()

        def some(g, carry):
            cut = pl.ds(pl.multiple_of(g * group, 8), group)
            value = amp[c, cut, :]
            act = jnp.dot(
                act_ref[0], value, precision=lax.Precision.HIGHEST, preferred_element_type=F32
            ) + jnp.dot(
                act_ref[1], turn(value, pairs), precision=lax.Precision.HIGHEST,
                preferred_element_type=F32,
            )
            total = kept[c, cut, :] + far_in[c, cut, :].astype(F32)
            den = den_ref[c, cut, :]
            source = src_ref[c, cut, :]
            fresh = (source - act - total) / den
            amp[c, cut, :] = fresh
            kept[c, cut, :] = fresh - jnp.where(final, source / den, 0.0)
            return carry

        lax.fori_loop(0, tile // group, some, 0)
        out = kept[c].astype(BF16)
        x_ref[c, fit] = out
        gather_across(c, fit).start()
        gather_beside(c, fit).start()

        @pl.when(jnp.logical_not(final))
        def _():
            ring[parity, vir, c] = out
            open_ring(parity, c)

    def pass_on(c):
        gather_across(c, across).wait_recv()
        gather_relay(c, across).start()

    def gathered(c):
        gather_beside(c, beside).wait_recv()
        gather_relay(c, order[0]).wait_recv()

    def back_sends(c):
        for k in range(2):
            near_copy(c, k).wait_send()
        far_copy(c).wait_send()
        gather_across(c, fit).wait_send()
        gather_beside(c, fit).wait_send()
        gather_relay(c, across).wait_send()

    for c in range(chunks):
        open_ring(0, c)

    contract = (((0,), (0,)), ((), ()))
    last_chunk = chunks - 1

    def one_pass(p, carry):
        parity = lax.rem(p, 2)
        later = p > 0
        acc[...] = jnp.zeros_like(acc)

        def contract_step(i, carry):
            ahead = i + SLOTS - 1
            inside = ahead < tiles
            target = jnp.where(inside, ahead, back_tile(ahead - tiles))
            fetch(target, lax.rem(ahead, SLOTS)).start()
            c = i // n_fit
            j = lax.rem(i, n_fit)

            @pl.when(later & (j == 0))
            def _():
                gathered(c)

            slot = lax.rem(i, SLOTS)
            fetch(i, slot).wait()
            values = x_ref[c, j]
            acc[...] += lax.dot_general(
                values, buf[slot, 0], contract, preferred_element_type=F32
            ) + lax.dot_general(
                -turn(values, pairs), buf[slot, 1], contract, preferred_element_type=F32
            )

            @pl.when(later & (i == 2))
            def _():
                update(last_chunk, parity, False)

            @pl.when(later & ((i == 1) | (i == 5)))
            def _():
                pass_on(jnp.where(i == 1, last_chunk - 1, last_chunk))

            code = jnp.where(later, choose_int(i, LATER_RELAYS), choose_int(i, FIRST_RELAYS))

            @pl.when(code > 0)
            def _():
                relay(parity, code // 8, lax.rem(code, 8))

            return carry

        lax.fori_loop(0, tiles, contract_step, 0)

        for k in range(n):
            part[k] = acc[k * band : (k + 1) * band, :].astype(BF16)
        for k in range(1, n):
            part_copy(k).start()

        @pl.when(later)
        def _():
            for c in range(chunks):
                back_sends(c)

        for c in range(chunks):
            lay(parity, vir, c)
        for c in range(chunks):
            lay(parity, landed(parity, 0 if c < split else 1, half, c), c)
        total = acc[pl.ds(pl.multiple_of(vir * band, band), band), :]
        for k in range(1, n):
            total = total + parts[part_landed(k)].astype(F32)
        whole[vir] = total.astype(BF16)
        for k in range(1, n):
            whole_copy(k).start()

        for t in range(0, active, 2):
            left = rows[:, t * lanes : (t + 1) * lanes]
            right = rows[:, (t + 1) * lanes : (t + 2) * lanes]
            plain = jnp.concatenate([left, right], axis=1)
            other = jnp.concatenate([turn(left, pairs), turn(right, pairs)], axis=1)
            value = plain_product(couple_ref[0], plain) + plain_product(couple_ref[1], other)
            virtual[:, t, :] = value[:, :lanes]
            virtual[:, t + 1, :] = value[:, lanes:]

        for c in range(chunks):
            for side in range(2):
                for stage in range(1, half + 1):
                    if stage < half or sent_last(side, c):
                        hop(parity, side, stage, c).wait_send()
        for k in range(1, n):
            whole_landed(k)
        block = depth
        for width in (512, 384, 256, 128):
            if depth % width == 0:
                block = width
                break
        for q in range(0, depth, block):
            cols = whole[:, :, q : q + block].reshape(lanes, block).astype(F32).T
            inter[q : q + block, :] = cols.astype(BF16)
            turned[q : q + block, :] = turn(cols, pairs).astype(BF16)
        for k in range(1, n):
            part_copy(k).wait_send()
            whole_copy(k).wait_send()

        final = p == PASSES - 1
        own = tile // active

        def back_chunk(c, carry):
            for k in range(n_fit):
                i = c * n_fit + k
                ahead = i + SLOTS - 1
                inside = ahead < tiles
                after = ahead - tiles
                target = jnp.where(
                    inside, (ahead // n_fit) * n_fit + order[(k + SLOTS - 1) % n_fit], after
                )

                @pl.when(inside | jnp.logical_not(final))
                def _():
                    fetch(target, lax.rem(ahead, SLOTS)).start()

                slot = lax.rem(i, SLOTS)
                where = c * n_fit + order[k]
                fetch(where, slot).wait()
                value = (
                    plain_product(buf[slot, 0], inter[...])
                    + plain_product(buf[slot, 1], turned[...])
                    + virtual[pl.ds(where * own, own)].reshape(tile, lanes)
                )
                if k < 2:
                    near[c, k] = value.astype(BF16)
                    near_copy(c, k).start()
                elif k == 2:
                    near_copy(c, 0).wait_recv()
                    far[c] = (value + near_in[c, 0].astype(F32)).astype(BF16)
                    far_copy(c).start()
                else:
                    near_copy(c, 1).wait_recv()
                    kept[c] = value + near_in[c, 1].astype(F32)
                if k == 0:

                    @pl.when(c >= 2)
                    def _():
                        pass_on(c - 2)

                    @pl.when((c >= 2) & jnp.logical_not(final))
                    def _():
                        relay(1 - parity, 1, c - 2)

                if k == 1:

                    @pl.when(c >= 1)
                    def _():
                        update(c - 1, 1 - parity, final)

                if k == 3:

                    @pl.when((c >= 2) & jnp.logical_not(final))
                    def _():
                        relay(1 - parity, 2, c - 2)

            return carry

        lax.fori_loop(0, chunks, back_chunk, 0)
        return carry

    lax.fori_loop(0, PASSES, one_pass, 0)
    pass_on(last_chunk - 1)
    update(last_chunk, 0, True)
    pass_on(last_chunk)
    for c in range(chunks):
        gathered(c)
        back_sends(c)


FIRST_RELAYS = {1: 8, 2: 9, 3: 10, 5: 16, 6: 17, 7: 18, 9: 24, 10: 25, 11: 26}
LATER_RELAYS = {0: 9, 3: 24, 4: 17, 6: 10, 7: 25, 8: 18, 10: 26}


def all_passes(fit_rows, values, couple, src, den, act, active, n):
    depth = fit_rows.shape[2]
    chunks, n_fit, tile, lanes = values.shape
    local_vir, wide = couple.shape[1:]
    span = wide // (chunks * n)
    half = n // 2
    dma = pltpu.SemaphoreType.DMA
    band = pltpu.VMEM((n, lanes // n, depth), BF16)
    each = pltpu.VMEM((chunks, tile, lanes), BF16)
    twice = pltpu.VMEM((chunks, 2, tile, lanes), BF16)
    state = pltpu.VMEM((chunks, tile, lanes), F32)
    return pl.pallas_call(
        lambda *refs: passes_kernel(n, *refs),
        in_specs=[pl.BlockSpec(memory_space=pl.ANY)] + whole_vmem(5),
        out_specs=pl.BlockSpec(memory_space=pltpu.VMEM),
        out_shape=jax.ShapeDtypeStruct((chunks, n_fit, tile, lanes), BF16),
        scratch_shapes=[
            pltpu.VMEM((SLOTS, 2, tile, depth), BF16),
            dma((SLOTS,)),
            pltpu.VMEM((lanes, depth), F32),
            band,
            band,
            band,
            pltpu.VMEM((depth, lanes), BF16),
            pltpu.VMEM((depth, lanes), BF16),
            pltpu.VMEM((2, n, chunks, tile, lanes), BF16),
            pltpu.VMEM((span * active, lanes), F32),
            pltpu.VMEM((wide, active * lanes), BF16),
            pltpu.VMEM((local_vir, active, lanes), F32),
            twice,
            twice,
            each,
            each,
            state,
            state,
            dma((2, half, chunks)),
            dma((2, half, chunks)),
        ]
        + [dma((n - 1,))] * 4
        + [dma((2, chunks))]
        + [dma((chunks, 2))] * 2
        + [dma((chunks,))] * 8,
        compiler_params=pltpu.CompilerParams(
            collective_id=0, has_side_effects=True, vmem_limit_bytes=60 * 2**20
        ),
        name="passes",
    )(fit_rows, values, couple, src, den, act)


def per_device(fitted, vcouple, actfock, eps_vir, eps_act, pair_energy, source):
    n_fit, n_vir = lax.axis_size("fit"), lax.axis_size("vir")
    vir_index = lax.axis_index("vir")
    local_vir, active, local_fit = fitted.shape[1:]
    block_rows = vcouple.shape[1]
    pairs = pair_energy.shape[0]
    lanes = 2 * pairs
    own = local_vir // (CHUNKS * n_fit)
    span = -(-own // 16) * 16
    held = block_rows // local_vir

    row = eps_act[:, None] - pair_energy[None, :]
    wide_row = jnp.concatenate([row, row], axis=1)
    values, src, den = prologue(eps_vir, wide_row, source, n_fit)

    couple = lax.dynamic_slice_in_dim(vcouple, vir_index * local_vir, local_vir, 2)
    couple = couple.reshape(2, held, CHUNKS, n_fit, own, local_vir).transpose(3, 0, 1, 2, 4, 5)
    couple = couple.reshape(n_fit, 2 * held * CHUNKS * own, local_vir)
    couple = lax.all_to_all(couple, "fit", 0, 0)
    couple = couple.reshape(n_fit, 2, held, CHUNKS, own, local_vir).transpose(1, 5, 3, 0, 2, 4)
    couple = jnp.pad(couple, ((0, 0),) * 5 + ((0, span - own),))
    couple = couple.reshape(2, local_vir, CHUNKS * n_vir * span)

    group = 5
    eye = jnp.eye(group, dtype=F32)
    act = jnp.einsum("gh,cut->cgthu", eye, actfock).reshape(2, group * active, group * active)
    fit_rows = fitted.reshape(2, local_vir * active, local_fit)
    values = all_passes(fit_rows, values, couple, src, den, act, active, n_vir)
    change = values.reshape(CHUNKS * n_fit, own * active, lanes)
    return epilogue(eps_vir, row.reshape(1, active * pairs), source, change, active, lanes)


def choose(mesh):
    def body(*args):
        n_fit, n_vir = mesh.shape["fit"], mesh.shape["vir"]
        fitted, vcouple, actfock, eps_vir, eps_act, pair_energy, source = args
        local_vir, active, local_fit = fitted.shape[1:]
        fits = (
            n_fit == 4
            and CHUNKS == 3
            and n_vir == 8
            and n_vir % 2 == 0
            and 2 * pair_energy.shape[0] == 128
            and n_vir * 16 == 128
            and local_vir % (CHUNKS * n_fit * 5) == 0
            and vcouple.shape[1] % local_vir == 0
            and active % 8 == 0
            and local_fit % 128 == 0
        )
        return per_device(*args) if fits else plain_device(*args)

    return body


def solution(mesh):
    return jax.shard_map(
        choose(mesh),
        mesh=mesh,
        in_specs=(
            P(None, "vir", None, "fit"),
            P(None, "fit", None),
            P(),
            P("vir"),
            P(),
            P(),
            P(None, "vir", None),
        ),
        out_specs=P(None, "vir", None),
        check_vma=False,
    )
```

```python
import jax
import jax.numpy as jnp
from jax import lax
from jax.experimental import pallas as pl
from jax.experimental.pallas import tpu as pltpu
from jax.sharding import PartitionSpec as P

PASSES = 3
CHUNKS = 3
SLOTS = 3
BF16 = jnp.bfloat16
F32 = jnp.float32
MESH = pl.DeviceIdType.MESH

def contract_first(left, right):
    return lax.dot_general(
        left, right, (((0,), (0,)), ((), ())), preferred_element_type=jnp.float32
    )


def plain_product(left, right):
    return jnp.dot(left, right, preferred_element_type=jnp.float32)


def active_coupling(values, actfock, active, pairs):
    highest = lax.Precision.HIGHEST
    local_vir = values.shape[1]
    grid = values.reshape(2, local_vir, active, pairs)
    act_real = jnp.einsum("aup,ut->atp", grid[0], actfock[0], precision=highest) - jnp.einsum(
        "aup,ut->atp", grid[1], actfock[1], precision=highest
    )
    act_imag = jnp.einsum("aup,ut->atp", grid[0], actfock[1], precision=highest) + jnp.einsum(
        "aup,ut->atp", grid[1], actfock[0], precision=highest
    )
    return jnp.stack([act_real, act_imag]).reshape(2, local_vir, actfock.shape[2] * pairs)


def plain_device(fitted, vcouple, actfock, eps_vir, eps_act, pair_energy, source):
    local_vir = fitted.shape[1]
    active = fitted.shape[2]
    local_fit = fitted.shape[3]
    pairs = pair_energy.shape[0]
    block_rows = vcouple.shape[1]
    width = local_vir * active
    fit_index = lax.axis_index("fit")
    denominator = (
        eps_vir[:, None, None] + eps_act[None, :, None] - pair_energy[None, None, :]
    ).reshape(local_vir, active * pairs)
    amplitude = source / denominator[None]
    fit_real = fitted[0].reshape(width, local_fit)
    fit_imag = fitted[1].reshape(width, local_fit)
    for pass_index in range(PASSES):
        rounded = amplitude.astype(jnp.bfloat16)
        flat_both = jnp.concatenate(
            [rounded[0].reshape(width, pairs), rounded[1].reshape(width, pairs)], axis=1
        )
        real_side = contract_first(fit_real, flat_both)
        imag_side = contract_first(fit_imag, flat_both)
        over_real = real_side[:, :pairs] + imag_side[:, pairs:]
        over_imag = real_side[:, pairs:] - imag_side[:, :pairs]
        intersection = lax.psum(jnp.concatenate([over_real, over_imag], axis=1), "vir").astype(
            jnp.bfloat16
        )
        real_out = plain_product(fit_real, intersection)
        imag_out = plain_product(fit_imag, intersection)
        sum_real = real_out[:, :pairs] - imag_out[:, pairs:]
        sum_imag = real_out[:, pairs:] + imag_out[:, :pairs]
        fitted_part = jnp.stack([sum_real, sum_imag]).reshape(2, local_vir, active * pairs)
        regrouped = lax.all_to_all(rounded, "vir", split_axis=2, concat_axis=1, tiled=True)
        window = lax.dynamic_slice_in_dim(regrouped, fit_index * block_rows, block_rows, 1)
        couple_real = contract_first(vcouple[0], window[0]) - contract_first(vcouple[1], window[1])
        couple_imag = contract_first(vcouple[1], window[0]) + contract_first(vcouple[0], window[1])
        coupled = jnp.stack([couple_real, couple_imag])
        returned = lax.all_to_all(coupled, "vir", split_axis=1, concat_axis=2, tiled=True)
        fitted_part = fitted_part + returned
        total = lax.psum(fitted_part, "fit")
        part_amplitude = amplitude
        active_term = active_coupling(amplitude, actfock, active, pairs)
        residual = source - denominator[None] * part_amplitude - active_term - total
        updated = part_amplitude + residual / denominator[None]
        amplitude = updated
    return amplitude


def turn(values, pairs):
    return jnp.concatenate([-values[..., pairs:], values[..., :pairs]], axis=-1)


def whole_vmem(count):
    return [pl.BlockSpec(memory_space=pltpu.VMEM)] * count


def mix(values, pairs):
    rows, lanes = values.shape
    even = lax.broadcasted_iota(jnp.int32, (rows, lanes), 0) % 2 == 0
    low = lax.broadcasted_iota(jnp.int32, (rows, lanes), 1) < pairs
    other = pltpu.roll(values, pairs, 1)
    up = pltpu.roll(other, rows - 1, 0)
    down = pltpu.roll(other, 1, 0)
    return jnp.where(even == low, values, jnp.where(even, up, down))


def epilogue_kernel(eps_ref, row_ref, source_ref, change_ref, out_ref, den):
    tile, lanes = source_ref.shape
    active = row_ref.shape[0]
    own = tile // active
    first = pl.program_id(0) * own
    for i in range(own):
        den[i * active : (i + 1) * active, :] = eps_ref[pl.ds(first + i, 1), :] + row_ref[...]
    start = mix(source_ref[...], lanes // 2) / den[...]
    out_ref[...] = mix(start + change_ref[0].astype(F32), lanes // 2)


def epilogue(eps, row, source, change):
    pieces, tile, lanes = change.shape
    return pl.pallas_call(
        epilogue_kernel,
        grid=(pieces,),
        in_specs=[
            pl.BlockSpec(eps.shape, lambda i: (0, 0)),
            pl.BlockSpec(row.shape, lambda i: (0, 0)),
            pl.BlockSpec((tile, lanes), lambda i: (i, 0)),
            pl.BlockSpec((1, tile, lanes), lambda i: (i, 0, 0)),
        ],
        out_specs=pl.BlockSpec((tile, lanes), lambda i: (i, 0)),
        out_shape=jax.ShapeDtypeStruct(source.shape, F32),
        scratch_shapes=[pltpu.VMEM((tile, lanes), F32)],
        compiler_params=pltpu.CompilerParams(vmem_limit_bytes=16 * 2**20),
        name="epilogue",
    )(eps, row, source, change)


def ring_of(vir, n):
    odd = vir % 2
    return (1 - odd) * (vir // 2) + odd * (n - 1 - vir // 2)


def vir_of(pos, n):
    pos = (pos + n) % n
    high = pos // (n // 2)
    return (1 - high) * (2 * pos) + high * (2 * (n - 1 - pos) + 1)


def choose_int(index, table):
    value = 0
    for key, entry in table.items():
        value = value + jnp.where(index == key, entry, 0)
    return value


def passes_kernel(
    n, f_ref, source_ref, give_ref, eps_ref, row_ref, act_ref, x_ref,
    buf, buf_sem, acc, part, parts, whole, inter, turned, ring, spread, rows, virtual,
    near, near_in, far, far_in, kept, amp, src, inverse, base, raw, den, couple,
    ring_send, ring_recv, part_send, part_recv, whole_send, whole_recv, init_sem,
    couple_send, couple_recv,
    near_send, near_recv, far_send, far_recv, gx_send, gx_recv, gc_send, gc_recv, gr_send, gr_recv,
):
    vir, fit = lax.axis_index("vir"), lax.axis_index("fit")
    chunks, n_fit, tile, lanes = x_ref.shape
    pairs = lanes // 2
    tiles = chunks * n_fit
    band = lanes // n
    depth = acc.shape[1]
    active = virtual.shape[1]
    span = spread.shape[0] // active
    half = n // 2
    pos = ring_of(vir, n)
    sides = ((vir_of(pos + 1, n), 1), (vir_of(pos - 1, n), -1))
    x, core = fit // 2, fit % 2
    beside = x * 2 + (1 - core)
    across = (1 - x) * 2 + core
    order = ((1 - x) * 2 + (1 - core), beside, across, fit)
    split = (chunks + 1) // 2
    group = act_ref.shape[1]

    def fetch(row_tile, slot):
        row = pl.multiple_of(row_tile * tile, 8)
        return pltpu.make_async_copy(
            f_ref.at[:, pl.ds(row, tile), :], buf.at[slot], buf_sem.at[slot]
        )

    def remote(src, dst, send, recv, axis, peer):
        return pltpu.make_async_remote_copy(
            src_ref=src, dst_ref=dst, send_sem=send, recv_sem=recv,
            device_id={axis: peer}, device_id_type=MESH,
        )

    def back_tile(k):
        value = 0
        for j in range(n_fit):
            value = value + jnp.where(k == j, order[j], 0)
        return value

    for i in range(SLOTS - 1):
        fetch(i, i).start()
    own = tile // active
    raw_copies = [
        pltpu.make_async_copy(
            source_ref.at[pl.ds(pl.multiple_of((c * n_fit + fit) * tile, 8), tile), :],
            src.at[c], init_sem.at[0, c],
        )
        for c in range(chunks)
    ]
    for copy in raw_copies:
        copy.start()
    bulk = pltpu.make_async_copy(source_ref, raw, init_sem.at[1, 0])
    bulk.start()
    own_couple = pltpu.make_async_copy(give_ref.at[fit], couple.at[fit], init_sem.at[1, 1])
    own_couple.start()

    barrier = pltpu.get_barrier_semaphore()
    for k in range(1, n):
        pl.semaphore_signal(barrier, inc=1, device_id={"vir": (vir + k) % n}, device_id_type=MESH)
    for k in range(1, n_fit):
        pl.semaphore_signal(
            barrier, inc=1, device_id={"fit": (fit + k) % n_fit}, device_id_type=MESH
        )

    def fill(first):
        for i in range(own):
            den[i * active : (i + 1) * active, :] = eps_ref[pl.ds(first + i, 1), :] + row_ref[...]

    def begin(c, carry):
        fill((c * n_fit + fit) * own)
        source = mix(src[c], pairs)
        start = source / den[...]
        src[c] = source
        inverse[c] = 1.0 / den[...]
        amp[c] = start
        ring[0, vir, c] = start.astype(BF16)
        return carry

    for copy in raw_copies:
        copy.wait()
    lax.fori_loop(0, chunks, begin, 0)
    spread[...] = jnp.zeros_like(spread)
    pl.semaphore_wait(barrier, n + n_fit - 2)

    def sent_last(side, c):
        return (c < split) if side == 0 else (c >= split)

    def hop(parity, side, stage, c):
        to, sign = sides[side]
        owner = vir_of(pos - sign * (stage - 1), n)
        slot = ring.at[parity, owner, c]
        return remote(
            slot, slot, ring_send.at[side, stage - 1, c], ring_recv.at[side, stage - 1, c], "vir", to
        )

    def lay(parity, owner, c):
        spread[0:tile, :] = ring[parity, owner, c].astype(F32)
        top = pl.multiple_of((owner * chunks + c) * span, span)
        for t in range(active):
            rows[pl.ds(top, span), t * lanes : (t + 1) * lanes] = spread[
                pl.ds(t, span, stride=active), :
            ].astype(BF16)

    def landed(parity, side, stage, c):
        to, sign = sides[side]
        owner = vir_of(pos - sign * stage, n)
        slot = ring.at[parity, owner, c]
        remote(
            slot, slot, ring_send.at[side, stage - 1, c], ring_recv.at[side, stage - 1, c], "vir", to
        ).wait_recv()
        return owner

    def open_ring(parity, c):
        for side in range(2):
            hop(parity, side, 1, c).start()

    def relay(parity, stage, c):
        owners = []
        for side in range(2):
            owners.append(landed(parity, side, stage, c))

            @pl.when((stage < half - 1) | sent_last(side, c))
            def _():
                hop(parity, side, stage + 1, c).start()

        for owner in owners:
            lay(parity, owner, c)

    def part_copy(k):
        peer = (vir + k) % n
        return remote(
            part.at[peer], parts.at[vir], part_send.at[k - 1], part_recv.at[k - 1], "vir", peer
        )

    def part_landed(k):
        peer = (vir + n - k) % n
        remote(
            part.at[peer], parts.at[peer], part_send.at[k - 1], part_recv.at[k - 1], "vir", peer
        ).wait_recv()
        return peer

    def whole_copy(k):
        peer = (vir + k) % n
        return remote(
            whole.at[vir], whole.at[vir], whole_send.at[k - 1], whole_recv.at[k - 1], "vir", peer
        )

    def whole_landed(k):
        peer = (vir + n - k) % n
        remote(
            whole.at[peer], whole.at[peer], whole_send.at[k - 1], whole_recv.at[k - 1], "vir", peer
        ).wait_recv()

    def near_copy(c, k):
        return remote(
            near.at[c, k], near_in.at[c, k], near_send.at[c, k], near_recv.at[c, k], "fit", beside
        )

    def far_copy(c):
        return remote(far.at[c], far_in.at[c], far_send.at[c], far_recv.at[c], "fit", across)

    def gather_across(c, owner):
        slot = x_ref.at[c, owner]
        return remote(slot, slot, gx_send.at[c], gx_recv.at[c], "fit", across)

    def gather_beside(c, owner):
        slot = x_ref.at[c, owner]
        return remote(slot, slot, gc_send.at[c], gc_recv.at[c], "fit", beside)

    def gather_relay(c, owner):
        slot = x_ref.at[c, owner]
        return remote(slot, slot, gr_send.at[c], gr_recv.at[c], "fit", beside)

    def update(c, parity, final):
        far_copy(c).wait_recv()

        total = kept[c] + far_in[c].astype(F32)
        fresh = (base[c] - total) * inverse[c]
        amp[c] = fresh
        out = (fresh - jnp.where(final, src[c] * inverse[c], 0.0)).astype(BF16)
        x_ref[c, fit] = out
        gather_across(c, fit).start()
        gather_beside(c, fit).start()

        @pl.when(jnp.logical_not(final))
        def _():
            ring[parity, vir, c] = out
            open_ring(parity, c)

    def pass_on(c):
        gather_across(c, across).wait_recv()
        gather_relay(c, across).start()

    def gathered(c):
        gather_beside(c, beside).wait_recv()
        gather_relay(c, order[0]).wait_recv()

    def back_sends(c):
        for k in range(2):
            near_copy(c, k).wait_send()
        far_copy(c).wait_send()
        gather_across(c, fit).wait_send()
        gather_beside(c, fit).wait_send()
        gather_relay(c, across).wait_send()

    for c in range(chunks):
        open_ring(0, c)

    def couple_copy(k):
        peer = (fit + k) % n_fit
        return remote(
            give_ref.at[peer], couple.at[fit], couple_send.at[k - 1], couple_recv.at[k - 1], "fit", peer
        )

    def couple_landed(k):
        peer = (fit + n_fit - k) % n_fit
        remote(
            give_ref.at[peer], couple.at[peer], couple_send.at[k - 1], couple_recv.at[k - 1], "fit", peer
        ).wait_recv()

    for k in range(1, n_fit):
        couple_copy(k).start()

    def spread_start(i, carry):
        fill(i * own)
        source = raw[pl.ds(pl.multiple_of(i * tile, 8), tile), :]
        x_ref[i // n_fit, lax.rem(i, n_fit)] = (mix(source, pairs) / den[...]).astype(BF16)
        return carry

    bulk.wait()
    lax.fori_loop(0, tiles, spread_start, 0)

    def active_base(c, carry):
        value = amp[c]
        cuts = [value[g : g + group] for g in range(0, tile, group)]
        both = jnp.concatenate(
            [
                jnp.concatenate(cuts, axis=1),
                jnp.concatenate([turn(cut, pairs) for cut in cuts], axis=1),
            ],
            axis=0,
        )
        high = both.astype(BF16)
        low = (both - high.astype(F32)).astype(BF16)
        act = (
            plain_product(act_ref[0], high)
            + plain_product(act_ref[0], low)
            + plain_product(act_ref[1], high)
        )
        for g in range(tile // group):
            cut = slice(g * group, (g + 1) * group)
            base[c, cut, :] = src[c, cut, :] - act[:, g * lanes : (g + 1) * lanes]
        return carry

    contract = (((0,), (0,)), ((), ()))
    last_chunk = chunks - 1

    def one_pass(p, carry):
        parity = lax.rem(p, 2)
        later = p > 0
        acc[...] = jnp.zeros_like(acc)

        def contract_step(i, carry):
            ahead = i + SLOTS - 1
            inside = ahead < tiles
            target = jnp.where(inside, ahead, back_tile(ahead - tiles))
            fetch(target, lax.rem(ahead, SLOTS)).start()
            c = i // n_fit
            j = lax.rem(i, n_fit)

            @pl.when(later & (j == 0))
            def _():
                gathered(c)

            slot = lax.rem(i, SLOTS)
            fetch(i, slot).wait()
            values = x_ref[c, j]
            acc[...] += lax.dot_general(
                values, buf[slot, 0], contract, preferred_element_type=F32
            ) + lax.dot_general(
                -turn(values, pairs), buf[slot, 1], contract, preferred_element_type=F32
            )

            @pl.when(later & (i == 2))
            def _():
                update(last_chunk, parity, False)

            @pl.when(later & ((i == 1) | (i == 5)))
            def _():
                pass_on(jnp.where(i == 1, last_chunk - 1, last_chunk))

            code = jnp.where(later, choose_int(i, LATER_RELAYS), choose_int(i, FIRST_RELAYS))

            @pl.when(code > 0)
            def _():
                relay(parity, code // 8, lax.rem(code, 8))

            return carry

        lax.fori_loop(0, tiles, contract_step, 0)

        for k in range(n):
            part[k] = acc[k * band : (k + 1) * band, :].astype(BF16)
        for k in range(1, n):
            part_copy(k).start()

        @pl.when(later)
        def _():
            for c in range(chunks):
                back_sends(c)

        for c in range(chunks):
            lay(parity, vir, c)
        lax.fori_loop(0, chunks, active_base, 0)

        @pl.when(jnp.logical_not(later))
        def _():
            own_couple.wait()
            for k in range(1, n_fit):
                couple_landed(k)

        total = acc[pl.ds(pl.multiple_of(vir * band, band), band), :]
        for k in range(1, n):
            total = total + parts[part_landed(k)].astype(F32)
        whole[vir] = total.astype(BF16)
        for k in range(1, n):
            whole_copy(k).start()
        for c in range(chunks):
            lay(parity, landed(parity, 0 if c < split else 1, half, c), c)
        couple_parts = [
            jnp.concatenate([couple[j, part_index] for j in range(n_fit)], axis=0)
            for part_index in range(2)
        ]
        heights = virtual.shape[0]

        for t in range(0, active, 2):
            left = rows[:, t * lanes : (t + 1) * lanes]
            right = rows[:, (t + 1) * lanes : (t + 2) * lanes]
            plain = jnp.concatenate([left, right], axis=1)
            other = jnp.concatenate([turn(left, pairs), turn(right, pairs)], axis=1)
            value = contract_first(couple_parts[0], plain) + contract_first(couple_parts[1], other)
            virtual[:, t, :] = value[:heights, :lanes]
            virtual[:, t + 1, :] = value[:heights, lanes:]

        for c in range(chunks):
            for side in range(2):
                for stage in range(1, half + 1):
                    if stage < half or sent_last(side, c):
                        hop(parity, side, stage, c).wait_send()
        for k in range(1, n):
            whole_landed(k)
        block = depth
        for width in (512, 384, 256, 128):
            if depth % width == 0:
                block = width
                break
        for q in range(0, depth, block):
            cols = whole[:, :, q : q + block].reshape(lanes, block).astype(F32).T
            inter[q : q + block, :] = cols.astype(BF16)
            turned[q : q + block, :] = turn(cols, pairs).astype(BF16)
        for k in range(1, n):
            part_copy(k).wait_send()
            whole_copy(k).wait_send()

        final = p == PASSES - 1

        def back_chunk(c, carry):
            for k in range(n_fit):
                i = c * n_fit + k
                ahead = i + SLOTS - 1
                inside = ahead < tiles
                after = ahead - tiles
                target = jnp.where(
                    inside, (ahead // n_fit) * n_fit + order[(k + SLOTS - 1) % n_fit], after
                )

                @pl.when(inside | jnp.logical_not(final))
                def _():
                    fetch(target, lax.rem(ahead, SLOTS)).start()

                slot = lax.rem(i, SLOTS)
                where = c * n_fit + order[k]
                fetch(where, slot).wait()
                value = (
                    plain_product(buf[slot, 0], inter[...])
                    + plain_product(buf[slot, 1], turned[...])
                    + virtual[pl.ds(where * own, own)].reshape(tile, lanes)
                )
                if k < 2:
                    near[c, k] = value.astype(BF16)
                    near_copy(c, k).start()
                elif k == 2:
                    near_copy(c, 0).wait_recv()
                    far[c] = (value + near_in[c, 0].astype(F32)).astype(BF16)
                    far_copy(c).start()
                else:
                    near_copy(c, 1).wait_recv()
                    kept[c] = value + near_in[c, 1].astype(F32)
                if k == 0:

                    @pl.when(c >= 2)
                    def _():
                        pass_on(c - 2)

                    @pl.when((c >= 2) & jnp.logical_not(final))
                    def _():
                        relay(1 - parity, 1, c - 2)

                if k == 1:

                    @pl.when(c >= 1)
                    def _():
                        update(c - 1, 1 - parity, final)

                if k == 3:

                    @pl.when((c >= 2) & jnp.logical_not(final))
                    def _():
                        relay(1 - parity, 2, c - 2)

            return carry

        lax.fori_loop(0, chunks, back_chunk, 0)
        return carry

    lax.fori_loop(0, PASSES, one_pass, 0)
    pass_on(last_chunk - 1)
    update(last_chunk, 0, True)
    pass_on(last_chunk)
    for c in range(chunks):
        gathered(c)
        back_sends(c)
    for k in range(1, n_fit):
        couple_copy(k).wait_send()


FIRST_RELAYS = {1: 8, 2: 9, 3: 10, 5: 16, 6: 17, 7: 18, 9: 24, 10: 25, 11: 26}
LATER_RELAYS = {0: 9, 3: 24, 4: 17, 6: 10, 7: 25, 8: 18, 10: 26}


def all_passes(fit_rows, source, give, eps, row, act, n):
    depth = fit_rows.shape[2]
    active, lanes = row.shape
    n_fit, chunks = give.shape[0], CHUNKS
    local_vir = eps.shape[0]
    tile = local_vir // (chunks * n_fit) * active
    wide = n_fit * give.shape[2]
    span = wide // (chunks * n)
    half = n // 2
    dma = pltpu.SemaphoreType.DMA
    band = pltpu.VMEM((n, lanes // n, depth), BF16)
    each = pltpu.VMEM((chunks, tile, lanes), BF16)
    twice = pltpu.VMEM((chunks, 2, tile, lanes), BF16)
    state = pltpu.VMEM((chunks, tile, lanes), F32)
    any_space = pl.BlockSpec(memory_space=pl.ANY)
    return pl.pallas_call(
        lambda *refs: passes_kernel(n, *refs),
        in_specs=[any_space, any_space] + whole_vmem(4),
        out_specs=pl.BlockSpec(memory_space=pltpu.VMEM),
        out_shape=jax.ShapeDtypeStruct((chunks, n_fit, tile, lanes), BF16),
        scratch_shapes=[
            pltpu.VMEM((SLOTS, 2, tile, depth), BF16),
            dma((SLOTS,)),
            pltpu.VMEM((lanes, depth), F32),
            band,
            band,
            band,
            pltpu.VMEM((depth, lanes), BF16),
            pltpu.VMEM((depth, lanes), BF16),
            pltpu.VMEM((2, n, chunks, tile, lanes), BF16),
            pltpu.VMEM((span * active, lanes), F32),
            pltpu.VMEM((wide, active * lanes), BF16),
            pltpu.VMEM((local_vir, active, lanes), F32),
            twice,
            twice,
            each,
            each,
            state,
            state,
            state,
            state,
            state,
            pltpu.VMEM((local_vir * active, lanes), F32),
            pltpu.VMEM((tile, lanes), F32),
            pltpu.VMEM(give.shape, BF16),
            dma((2, half, chunks)),
            dma((2, half, chunks)),
        ]
        + [dma((n - 1,))] * 4
        + [dma((2, chunks))]
        + [dma((n_fit - 1,))] * 2
        + [dma((chunks, 2))] * 2
        + [dma((chunks,))] * 8,
        compiler_params=pltpu.CompilerParams(
            collective_id=0, has_side_effects=True, vmem_limit_bytes=60 * 2**20
        ),
        name="passes",
    )(fit_rows, source, give, eps, row, act)


def per_device(fitted, vcouple, actfock, eps_vir, eps_act, pair_energy, source):
    n_fit, n_vir = lax.axis_size("fit"), lax.axis_size("vir")
    vir_index = lax.axis_index("vir")
    local_vir, active, local_fit = fitted.shape[1:]
    block_rows = vcouple.shape[1]
    pairs = pair_energy.shape[0]
    lanes = 2 * pairs
    own = local_vir // (CHUNKS * n_fit)
    span = -(-own // 16) * 16
    held = block_rows // local_vir
    high = -(-local_vir // 128) * 128

    row = eps_act[:, None] - pair_energy[None, :]
    row = jnp.concatenate([row, row], axis=1)
    eps = jnp.broadcast_to(eps_vir[:, None], (local_vir, lanes))
    flat = source.reshape(2, local_vir, active // 2, lanes)
    flat = flat.transpose(1, 2, 0, 3).reshape(local_vir * active, lanes)

    give = lax.dynamic_slice_in_dim(vcouple, vir_index * local_vir, local_vir, 2)
    give = give.reshape(2, held, CHUNKS, n_fit, own, local_vir).transpose(3, 0, 1, 2, 4, 5)
    give = jnp.pad(give, ((0, 0),) * 4 + ((0, span - own), (0, high - local_vir)))
    give = give.reshape(n_fit, 2, held * CHUNKS * span, high)

    group = 5
    eye = jnp.eye(group, dtype=F32)
    act = jnp.einsum("gh,cut->gtchu", eye, actfock).reshape(group * active, 2 * group * active)
    act_high = act.astype(BF16)
    act_low = (act - act_high.astype(F32)).astype(BF16)
    act = jnp.stack([act_high, act_low])
    fit_rows = fitted.reshape(2, local_vir * active, local_fit)
    change = all_passes(fit_rows, flat, give, eps, row, act, n_vir)
    out = epilogue(eps, row, flat, change.reshape(CHUNKS * n_fit, own * active, lanes))
    out = out.reshape(local_vir, active // 2, 2, lanes).transpose(0, 2, 1, 3)
    return out.reshape(local_vir, 2, active * pairs).transpose(1, 0, 2)


def choose(mesh):
    def body(*args):
        n_fit, n_vir = mesh.shape["fit"], mesh.shape["vir"]
        fitted, vcouple, actfock, eps_vir, eps_act, pair_energy, source = args
        local_vir, active, local_fit = fitted.shape[1:]
        fits = (
            n_fit == 4
            and CHUNKS == 3
            and n_vir == 8
            and n_vir % 2 == 0
            and 2 * pair_energy.shape[0] == 128
            and n_vir * 16 == 128
            and local_vir % (CHUNKS * n_fit * 5) == 0
            and vcouple.shape[1] % local_vir == 0
            and active % 8 == 0
            and local_fit % 128 == 0
        )
        return per_device(*args) if fits else plain_device(*args)

    return body


def solution(mesh):
    return jax.shard_map(
        choose(mesh),
        mesh=mesh,
        in_specs=(
            P(None, "vir", None, "fit"),
            P(None, "fit", None),
            P(),
            P("vir"),
            P(),
            P(),
            P(None, "vir", None),
        ),
        out_specs=P(None, "vir", None),
        check_vma=False,
    )
```

```python
import jax
import jax.numpy as jnp
from jax import lax
from jax.experimental.layout import Layout, with_layout_constraint
from jax.experimental import pallas as pl
from jax.experimental.pallas import tpu as pltpu
from jax.sharding import PartitionSpec as P

PASSES = 3
CHUNKS = 3
SLOTS = 6
HALVES = 2
BF16 = jnp.bfloat16
F32 = jnp.float32
MESH = pl.DeviceIdType.MESH

def contract_first(left, right):
    return lax.dot_general(
        left, right, (((0,), (0,)), ((), ())), preferred_element_type=jnp.float32
    )


def plain_product(left, right):
    return jnp.dot(left, right, preferred_element_type=jnp.float32)


def active_coupling(values, actfock, active, pairs):
    highest = lax.Precision.HIGHEST
    local_vir = values.shape[1]
    grid = values.reshape(2, local_vir, active, pairs)
    act_real = jnp.einsum("aup,ut->atp", grid[0], actfock[0], precision=highest) - jnp.einsum(
        "aup,ut->atp", grid[1], actfock[1], precision=highest
    )
    act_imag = jnp.einsum("aup,ut->atp", grid[0], actfock[1], precision=highest) + jnp.einsum(
        "aup,ut->atp", grid[1], actfock[0], precision=highest
    )
    return jnp.stack([act_real, act_imag]).reshape(2, local_vir, actfock.shape[2] * pairs)


def plain_device(fitted, vcouple, actfock, eps_vir, eps_act, pair_energy, source):
    local_vir = fitted.shape[1]
    active = fitted.shape[2]
    local_fit = fitted.shape[3]
    pairs = pair_energy.shape[0]
    block_rows = vcouple.shape[1]
    width = local_vir * active
    fit_index = lax.axis_index("fit")
    denominator = (
        eps_vir[:, None, None] + eps_act[None, :, None] - pair_energy[None, None, :]
    ).reshape(local_vir, active * pairs)
    amplitude = source / denominator[None]
    fit_real = fitted[0].reshape(width, local_fit)
    fit_imag = fitted[1].reshape(width, local_fit)
    for pass_index in range(PASSES):
        rounded = amplitude.astype(jnp.bfloat16)
        flat_both = jnp.concatenate(
            [rounded[0].reshape(width, pairs), rounded[1].reshape(width, pairs)], axis=1
        )
        real_side = contract_first(fit_real, flat_both)
        imag_side = contract_first(fit_imag, flat_both)
        over_real = real_side[:, :pairs] + imag_side[:, pairs:]
        over_imag = real_side[:, pairs:] - imag_side[:, :pairs]
        intersection = lax.psum(jnp.concatenate([over_real, over_imag], axis=1), "vir").astype(
            jnp.bfloat16
        )
        real_out = plain_product(fit_real, intersection)
        imag_out = plain_product(fit_imag, intersection)
        sum_real = real_out[:, :pairs] - imag_out[:, pairs:]
        sum_imag = real_out[:, pairs:] + imag_out[:, :pairs]
        fitted_part = jnp.stack([sum_real, sum_imag]).reshape(2, local_vir, active * pairs)
        regrouped = lax.all_to_all(rounded, "vir", split_axis=2, concat_axis=1, tiled=True)
        window = lax.dynamic_slice_in_dim(regrouped, fit_index * block_rows, block_rows, 1)
        couple_real = contract_first(vcouple[0], window[0]) - contract_first(vcouple[1], window[1])
        couple_imag = contract_first(vcouple[1], window[0]) + contract_first(vcouple[0], window[1])
        coupled = jnp.stack([couple_real, couple_imag])
        returned = lax.all_to_all(coupled, "vir", split_axis=1, concat_axis=2, tiled=True)
        fitted_part = fitted_part + returned
        total = lax.psum(fitted_part, "fit")
        part_amplitude = amplitude
        active_term = active_coupling(amplitude, actfock, active, pairs)
        residual = source - denominator[None] * part_amplitude - active_term - total
        updated = part_amplitude + residual / denominator[None]
        amplitude = updated
    return amplitude


def turn(values, pairs):
    return jnp.concatenate([-values[..., pairs:], values[..., :pairs]], axis=-1)


def whole_vmem(count):
    return [pl.BlockSpec(memory_space=pltpu.VMEM)] * count


def mix(values, pairs):
    rows, lanes = values.shape
    even = lax.broadcasted_iota(jnp.int32, (rows, lanes), 0) % 2 == 0
    low = lax.broadcasted_iota(jnp.int32, (rows, lanes), 1) < pairs
    other = pltpu.roll(values, pairs, 1)
    up = pltpu.roll(other, rows - 1, 0)
    down = pltpu.roll(other, 1, 0)
    return jnp.where(even == low, values, jnp.where(even, up, down))


def epilogue_kernel(eps_ref, row_ref, source_ref, change_ref, out_ref, den):
    group, tile, lanes = change_ref.shape
    active = row_ref.shape[0]
    own = tile // active

    def one(j, carry):
        first = (pl.program_id(0) * group + j) * own
        for i in range(own):
            den[i * active : (i + 1) * active, :] = eps_ref[pl.ds(first + i, 1), :] + row_ref[...]
        cut = pl.ds(pl.multiple_of(j * tile, 8), tile)
        start = mix(source_ref[cut, :], lanes // 2) / den[...]
        out_ref[cut, :] = mix(start + change_ref[j].astype(F32), lanes // 2)
        return carry

    lax.fori_loop(0, group, one, 0)


def epilogue(eps, row, source, change):
    pieces, tile, lanes = change.shape
    return pl.pallas_call(
        epilogue_kernel,
        grid=(pieces // CHUNKS,),
        in_specs=[
            pl.BlockSpec(eps.shape, lambda i: (0, 0)),
            pl.BlockSpec(row.shape, lambda i: (0, 0)),
            pl.BlockSpec((CHUNKS * tile, lanes), lambda i: (i, 0)),
            pl.BlockSpec((CHUNKS, tile, lanes), lambda i: (i, 0, 0)),
        ],
        out_specs=pl.BlockSpec((CHUNKS * tile, lanes), lambda i: (i, 0)),
        out_shape=jax.ShapeDtypeStruct(source.shape, F32),
        scratch_shapes=[pltpu.VMEM((tile, lanes), F32)],
        compiler_params=pltpu.CompilerParams(vmem_limit_bytes=16 * 2**20),
        name="epilogue",
    )(eps, row, source, change)


def ring_of(vir, n):
    odd = vir % 2
    return (1 - odd) * (vir // 2) + odd * (n - 1 - vir // 2)


def vir_of(pos, n):
    pos = (pos + n) % n
    high = pos // (n // 2)
    return (1 - high) * (2 * pos) + high * (2 * (n - 1 - pos) + 1)


def choose_int(index, table):
    value = 0
    for key, entry in table.items():
        value = value + jnp.where(index == key, entry, 0)
    return value


def passes_kernel(
    n, f_ref, source_ref, give_ref, eps_ref, row_ref, act_ref, x_ref,
    buf, buf_sem, acc, part, parts, whole, inter, turned, ring, spread, rows, virtual,
    near, near_in, far, far_in, kept, amp, src, inverse, base, raw, den, couple,
    ring_send, ring_recv, part_send, part_recv, whole_send, whole_recv, init_sem,
    couple_send, couple_recv,
    near_send, near_recv, far_send, far_recv, gx_send, gx_recv, gc_send, gc_recv, gr_send, gr_recv,
):
    vir, fit = lax.axis_index("vir"), lax.axis_index("fit")
    chunks, n_fit, tile, lanes = x_ref.shape
    pairs = lanes // 2
    tiles = chunks * n_fit
    band = lanes // n
    depth = acc.shape[2]
    active = virtual.shape[1]
    span = spread.shape[0] // active
    half = n // 2
    pos = ring_of(vir, n)
    sides = ((vir_of(pos + 1, n), 1), (vir_of(pos - 1, n), -1))
    x, core = fit // 2, fit % 2
    beside = x * 2 + (1 - core)
    across = (1 - x) * 2 + core
    order = ((1 - x) * 2 + (1 - core), beside, across, fit)
    split = (chunks + 1) // 2
    group = act_ref.shape[1]

    def fetch(row_tile, side, slot):
        row = pl.multiple_of(row_tile * tile, 8)
        column = pl.multiple_of(side * depth, 128)
        return pltpu.make_async_copy(
            f_ref.at[:, pl.ds(row, tile), pl.ds(column, depth)], buf.at[slot], buf_sem.at[slot]
        )

    def remote(src, dst, send, recv, axis, peer):
        return pltpu.make_async_remote_copy(
            src_ref=src, dst_ref=dst, send_sem=send, recv_sem=recv,
            device_id={axis: peer}, device_id_type=MESH,
        )

    def back_tile(k):
        value = 0
        for j in range(n_fit):
            value = value + jnp.where(k == j, order[j], 0)
        return value

    def prefetch(g):
        ahead = g + SLOTS - 1
        phase = lax.rem(ahead // tiles, 2 * HALVES)
        i = lax.rem(ahead, tiles)
        k = lax.rem(i, n_fit)
        which = jnp.where(phase == 2 * HALVES - 1, i - k + back_tile(k), i)
        fetch(which, lax.rem(phase, HALVES), lax.rem(ahead, SLOTS)).start()

    for i in range(SLOTS - 1):
        fetch(i, 0, i).start()
    own = tile // active
    raw_copies = [
        pltpu.make_async_copy(
            source_ref.at[pl.ds(pl.multiple_of((c * n_fit + fit) * tile, 8), tile), :],
            src.at[c], init_sem.at[0, c],
        )
        for c in range(chunks)
    ]
    for copy in raw_copies:
        copy.start()
    bulk = pltpu.make_async_copy(source_ref, raw, init_sem.at[1, 0])
    bulk.start()
    own_couple = pltpu.make_async_copy(give_ref.at[fit], couple.at[fit], init_sem.at[1, 1])
    own_couple.start()

    barrier = pltpu.get_barrier_semaphore()
    for k in range(1, n):
        pl.semaphore_signal(barrier, inc=1, device_id={"vir": (vir + k) % n}, device_id_type=MESH)
    for k in range(1, n_fit):
        pl.semaphore_signal(
            barrier, inc=1, device_id={"fit": (fit + k) % n_fit}, device_id_type=MESH
        )

    def fill(first):
        for i in range(own):
            den[i * active : (i + 1) * active, :] = eps_ref[pl.ds(first + i, 1), :] + row_ref[...]

    def begin(c, carry):
        fill((c * n_fit + fit) * own)
        source = mix(src[c], pairs)
        start = source / den[...]
        src[c] = source
        inverse[c] = 1.0 / den[...]
        amp[c] = start
        ring[0, vir, c] = start.astype(BF16)
        return carry

    for copy in raw_copies:
        copy.wait()
    lax.fori_loop(0, chunks, begin, 0)
    spread[...] = jnp.zeros_like(spread)
    pl.semaphore_wait(barrier, n + n_fit - 2)

    def sent_last(side, c):
        return (c < split) if side == 0 else (c >= split)

    def hop(parity, side, stage, c):
        to, sign = sides[side]
        owner = vir_of(pos - sign * (stage - 1), n)
        slot = ring.at[parity, owner, c]
        return remote(
            slot, slot, ring_send.at[side, stage - 1, c], ring_recv.at[side, stage - 1, c], "vir", to
        )

    def lay(parity, owner, c):
        spread[0:tile, :] = ring[parity, owner, c].astype(F32)
        top = pl.multiple_of((owner * chunks + c) * span, span)
        for t in range(active):
            rows[pl.ds(top, span), t * lanes : (t + 1) * lanes] = spread[
                pl.ds(t, span, stride=active), :
            ].astype(BF16)

    def landed(parity, side, stage, c):
        to, sign = sides[side]
        owner = vir_of(pos - sign * stage, n)
        slot = ring.at[parity, owner, c]
        remote(
            slot, slot, ring_send.at[side, stage - 1, c], ring_recv.at[side, stage - 1, c], "vir", to
        ).wait_recv()
        return owner

    def open_ring(parity, c):
        for side in range(2):
            hop(parity, side, 1, c).start()

    def relay(parity, stage, c):
        owners = []
        for side in range(2):
            owners.append(landed(parity, side, stage, c))

            @pl.when((stage < half - 1) | sent_last(side, c))
            def _():
                hop(parity, side, stage + 1, c).start()

        for owner in owners:
            lay(parity, owner, c)

    def part_copy(h, k):
        peer = (vir + k) % n
        return remote(
            part.at[h, peer], parts.at[h, vir], part_send.at[h, k - 1], part_recv.at[h, k - 1],
            "vir", peer,
        )

    def part_landed(h, k):
        peer = (vir + n - k) % n
        remote(
            part.at[h, peer], parts.at[h, peer], part_send.at[h, k - 1], part_recv.at[h, k - 1],
            "vir", peer,
        ).wait_recv()
        return peer

    def whole_copy(h, k):
        peer = (vir + k) % n
        slot = whole.at[h, vir]
        return remote(slot, slot, whole_send.at[h, k - 1], whole_recv.at[h, k - 1], "vir", peer)

    def whole_landed(h, k):
        peer = (vir + n - k) % n
        slot = whole.at[h, peer]
        remote(slot, slot, whole_send.at[h, k - 1], whole_recv.at[h, k - 1], "vir", peer).wait_recv()

    def give_parts(h):
        for k in range(n):
            part[h, k] = acc[h, k * band : (k + 1) * band, :].astype(BF16)
        for k in range(1, n):
            part_copy(h, k).start()

    def sum_parts(h):
        total = acc[h, pl.ds(pl.multiple_of(vir * band, band), band), :]
        for k in range(1, n):
            total = total + parts[h, part_landed(h, k)].astype(F32)
        whole[h, vir] = total.astype(BF16)
        for k in range(1, n):
            whole_copy(h, k).start()

    def take_whole(h):
        for k in range(1, n):
            whole_landed(h, k)
        cols = whole[h].reshape(lanes, depth).astype(F32).T
        inter[h] = cols.astype(BF16)
        turned[h] = turn(cols, pairs).astype(BF16)

    def near_copy(c, k):
        return remote(
            near.at[c, k], near_in.at[c, k], near_send.at[c, k], near_recv.at[c, k], "fit", beside
        )

    def far_copy(c):
        return remote(far.at[c], far_in.at[c], far_send.at[c], far_recv.at[c], "fit", across)

    def gather_across(c, owner):
        slot = x_ref.at[c, owner]
        return remote(slot, slot, gx_send.at[c], gx_recv.at[c], "fit", across)

    def gather_beside(c, owner):
        slot = x_ref.at[c, owner]
        return remote(slot, slot, gc_send.at[c], gc_recv.at[c], "fit", beside)

    def gather_relay(c, owner):
        slot = x_ref.at[c, owner]
        return remote(slot, slot, gr_send.at[c], gr_recv.at[c], "fit", beside)

    def update(c, parity, final):
        far_copy(c).wait_recv()

        total = kept[c] + far_in[c].astype(F32)
        fresh = (base[c] - total) * inverse[c]
        amp[c] = fresh
        out = (fresh - jnp.where(final, src[c] * inverse[c], 0.0)).astype(BF16)
        x_ref[c, fit] = out
        gather_across(c, fit).start()
        gather_beside(c, fit).start()

        @pl.when(jnp.logical_not(final))
        def _():
            ring[parity, vir, c] = out
            open_ring(parity, c)

    def pass_on(c):
        gather_across(c, across).wait_recv()
        gather_relay(c, across).start()

    def gathered(c):
        gather_beside(c, beside).wait_recv()
        gather_relay(c, order[0]).wait_recv()

    def back_sends(c):
        for k in range(2):
            near_copy(c, k).wait_send()
        far_copy(c).wait_send()
        gather_across(c, fit).wait_send()
        gather_beside(c, fit).wait_send()
        gather_relay(c, across).wait_send()

    for c in range(chunks):
        open_ring(0, c)

    def couple_copy(k):
        peer = (fit + k) % n_fit
        return remote(
            give_ref.at[peer], couple.at[fit], couple_send.at[k - 1], couple_recv.at[k - 1], "fit", peer
        )

    def couple_landed(k):
        peer = (fit + n_fit - k) % n_fit
        remote(
            give_ref.at[peer], couple.at[peer], couple_send.at[k - 1], couple_recv.at[k - 1], "fit", peer
        ).wait_recv()

    for k in range(1, n_fit):
        couple_copy(k).start()

    def spread_start(i, carry):
        fill(i * own)
        source = raw[pl.ds(pl.multiple_of(i * tile, 8), tile), :]
        x_ref[i // n_fit, lax.rem(i, n_fit)] = (mix(source, pairs) / den[...]).astype(BF16)
        return carry

    bulk.wait()
    lax.fori_loop(0, tiles, spread_start, 0)

    def active_base(c, carry):
        value = amp[c]
        cuts = [value[g : g + group] for g in range(0, tile, group)]
        both = jnp.concatenate(
            [
                jnp.concatenate(cuts, axis=1),
                jnp.concatenate([turn(cut, pairs) for cut in cuts], axis=1),
            ],
            axis=0,
        )
        high = both.astype(BF16)
        low = (both - high.astype(F32)).astype(BF16)
        act = (
            plain_product(act_ref[0], high)
            + plain_product(act_ref[0], low)
            + plain_product(act_ref[1], high)
        )
        for g in range(tile // group):
            cut = slice(g * group, (g + 1) * group)
            base[c, cut, :] = src[c, cut, :] - act[:, g * lanes : (g + 1) * lanes]
        return carry

    contract = (((0,), (0,)), ((), ()))
    last_chunk = chunks - 1

    def one_pass(p, carry):
        parity = lax.rem(p, 2)
        later = p > 0
        acc[...] = jnp.zeros_like(acc)

        def scheduled(g):
            code = jnp.where(later, choose_int(g, LATER_RELAYS), choose_int(g, FIRST_RELAYS))

            @pl.when(code > 0)
            def _():
                relay(parity, code // 8, lax.rem(code, 8))

        @pl.when(later)
        def _():
            update(last_chunk - 1, parity, False)
            pass_on(0)

        def contract_step(g, carry):
            prefetch(g)
            h = g // tiles
            i = lax.rem(g, tiles)
            c = i // n_fit
            j = lax.rem(i, n_fit)

            @pl.when(later & (h == 0) & (j == 0))
            def _():
                gathered(c)

            slot = lax.rem(g, SLOTS)
            fetch(i, h, slot).wait()
            values = x_ref[c, j]
            acc[h] += lax.dot_general(
                values, buf[slot, 0], contract, preferred_element_type=F32
            ) + lax.dot_general(
                -turn(values, pairs), buf[slot, 1], contract, preferred_element_type=F32
            )

            @pl.when(later & (g == 0))
            def _():
                update(last_chunk, parity, False)

            @pl.when(later & ((g == 2) | (g == 6)))
            def _():
                pass_on(jnp.where(g == 2, last_chunk - 1, last_chunk))

            @pl.when(g == tiles - 1)
            def _():
                give_parts(0)

            @pl.when(g == FIRST_SUM)
            def _():
                sum_parts(0)

            scheduled(g)
            return carry

        lax.fori_loop(0, HALVES * tiles, contract_step, 0)
        give_parts(1)

        @pl.when(later)
        def _():
            for c in range(chunks):
                back_sends(c)

        for c in range(chunks):
            lay(parity, vir, c)
        lax.fori_loop(0, chunks, active_base, 0)

        @pl.when(jnp.logical_not(later))
        def _():
            own_couple.wait()
            for k in range(1, n_fit):
                couple_landed(k)

        take_whole(0)

        def first_back(i, carry):
            g = HALVES * tiles + i
            prefetch(g)
            slot = lax.rem(g, SLOTS)
            fetch(i, 0, slot).wait()
            value = plain_product(buf[slot, 0], inter[0]) + plain_product(buf[slot, 1], turned[0])
            virtual[pl.ds(i * own, own)] = value.reshape(own, active, lanes)

            @pl.when(i == SECOND_SUM)
            def _():
                sum_parts(1)

            scheduled(g)
            return carry

        lax.fori_loop(0, tiles, first_back, 0)
        for c in range(chunks):
            lay(parity, landed(parity, 0 if c < split else 1, half, c), c)
        couple_parts = [
            jnp.concatenate([couple[j, part_index] for j in range(n_fit)], axis=0)
            for part_index in range(2)
        ]
        heights = virtual.shape[0]

        for t in range(0, active, 2):
            left = rows[:, t * lanes : (t + 1) * lanes]
            right = rows[:, (t + 1) * lanes : (t + 2) * lanes]
            plain = jnp.concatenate([left, right], axis=1)
            other = jnp.concatenate([turn(left, pairs), turn(right, pairs)], axis=1)
            value = contract_first(couple_parts[0], plain) + contract_first(couple_parts[1], other)
            virtual[:, t, :] += value[:heights, :lanes]
            virtual[:, t + 1, :] += value[:heights, lanes:]

        for c in range(chunks):
            for side in range(2):
                for stage in range(1, half + 1):
                    if stage < half or sent_last(side, c):
                        hop(parity, side, stage, c).wait_send()
        take_whole(1)
        for h in range(HALVES):
            for k in range(1, n):
                part_copy(h, k).wait_send()
                whole_copy(h, k).wait_send()

        final = p == PASSES - 1

        def back_chunk(c, carry):
            for k in range(n_fit):
                i = c * n_fit + k
                g = (HALVES + 1) * tiles + i

                @pl.when((i + SLOTS - 1 < tiles) | jnp.logical_not(final))
                def _():
                    prefetch(g)

                slot = lax.rem(g, SLOTS)
                where = c * n_fit + order[k]
                fetch(where, 1, slot).wait()
                value = (
                    plain_product(buf[slot, 0], inter[1])
                    + plain_product(buf[slot, 1], turned[1])
                    + virtual[pl.ds(where * own, own)].reshape(tile, lanes)
                )
                if k < 2:
                    near[c, k] = value.astype(BF16)
                    near_copy(c, k).start()
                elif k == 2:
                    near_copy(c, 0).wait_recv()
                    far[c] = (value + near_in[c, 0].astype(F32)).astype(BF16)
                    far_copy(c).start()
                else:
                    near_copy(c, 1).wait_recv()
                    kept[c] = value + near_in[c, 1].astype(F32)
                if k == 0:

                    @pl.when(c == 2)
                    def _():
                        update(0, 1 - parity, final)

            return carry

        lax.fori_loop(0, chunks, back_chunk, 0)
        return carry

    lax.fori_loop(0, PASSES, one_pass, 0)
    update(last_chunk - 1, 0, True)
    pass_on(0)
    update(last_chunk, 0, True)
    pass_on(last_chunk - 1)
    pass_on(last_chunk)
    for c in range(chunks):
        gathered(c)
        back_sends(c)
    for k in range(1, n_fit):
        couple_copy(k).wait_send()


FIRST_RELAYS = {5: 8, 9: 9, 13: 10, 17: 16, 20: 17, 23: 18, 27: 24, 30: 25, 33: 26}
LATER_RELAYS = {1: 8, 3: 9, 7: 16, 9: 10, 12: 17, 16: 24, 20: 18, 24: 25, 28: 26}
FIRST_SUM = 20
SECOND_SUM = 6


def all_passes(fit_rows, source, give, eps, row, act, n):
    depth = fit_rows.shape[2] // HALVES
    active, lanes = row.shape
    n_fit, chunks = give.shape[0], CHUNKS
    local_vir = eps.shape[0]
    tile = local_vir // (chunks * n_fit) * active
    wide = n_fit * give.shape[2]
    span = wide // (chunks * n)
    half = n // 2
    dma = pltpu.SemaphoreType.DMA
    band = pltpu.VMEM((HALVES, n, lanes // n, depth), BF16)
    each = pltpu.VMEM((chunks, tile, lanes), BF16)
    twice = pltpu.VMEM((chunks, 2, tile, lanes), BF16)
    state = pltpu.VMEM((chunks, tile, lanes), F32)
    any_space = pl.BlockSpec(memory_space=pl.ANY)
    return pl.pallas_call(
        lambda *refs: passes_kernel(n, *refs),
        in_specs=[any_space, any_space] + whole_vmem(4),
        out_specs=pl.BlockSpec(memory_space=pltpu.VMEM),
        out_shape=jax.ShapeDtypeStruct((chunks, n_fit, tile, lanes), BF16),
        scratch_shapes=[
            pltpu.VMEM((SLOTS, 2, tile, depth), BF16),
            dma((SLOTS,)),
            pltpu.VMEM((HALVES, lanes, depth), F32),
            band,
            band,
            band,
            pltpu.VMEM((HALVES, depth, lanes), BF16),
            pltpu.VMEM((HALVES, depth, lanes), BF16),
            pltpu.VMEM((2, n, chunks, tile, lanes), BF16),
            pltpu.VMEM((span * active, lanes), F32),
            pltpu.VMEM((wide, active * lanes), BF16),
            pltpu.VMEM((local_vir, active, lanes), F32),
            twice,
            twice,
            each,
            each,
            state,
            state,
            state,
            state,
            state,
            pltpu.VMEM((local_vir * active, lanes), F32),
            pltpu.VMEM((tile, lanes), F32),
            pltpu.VMEM(give.shape, BF16),
            dma((2, half, chunks)),
            dma((2, half, chunks)),
        ]
        + [dma((HALVES, n - 1))] * 4
        + [dma((2, chunks))]
        + [dma((n_fit - 1,))] * 2
        + [dma((chunks, 2))] * 2
        + [dma((chunks,))] * 8,
        compiler_params=pltpu.CompilerParams(
            collective_id=0, has_side_effects=True, vmem_limit_bytes=60 * 2**20
        ),
        name="passes",
    )(fit_rows, source, give, eps, row, act)


def per_device(fitted, vcouple, actfock, eps_vir, eps_act, pair_energy, source):
    n_fit, n_vir = lax.axis_size("fit"), lax.axis_size("vir")
    vir_index = lax.axis_index("vir")
    local_vir, active, local_fit = fitted.shape[1:]
    block_rows = vcouple.shape[1]
    pairs = pair_energy.shape[0]
    lanes = 2 * pairs
    own = local_vir // (CHUNKS * n_fit)
    span = -(-own // 16) * 16
    held = block_rows // local_vir
    high = -(-local_vir // 128) * 128

    row = eps_act[:, None] - pair_energy[None, :]
    row = jnp.concatenate([row, row], axis=1)
    eps = jnp.broadcast_to(eps_vir[:, None], (local_vir, lanes))
    flat = source.reshape(2, local_vir, active // 2, lanes)
    flat = with_layout_constraint(flat, Layout(major_to_minor=(1, 2, 0, 3)))
    flat = flat.transpose(1, 2, 0, 3).reshape(local_vir * active, lanes)

    give = lax.dynamic_slice_in_dim(vcouple, vir_index * local_vir, local_vir, 2)
    give = give.reshape(2, held, CHUNKS, n_fit, own, local_vir).transpose(3, 0, 1, 2, 4, 5)
    give = jnp.pad(give, ((0, 0),) * 4 + ((0, span - own), (0, high - local_vir)))
    give = give.reshape(n_fit, 2, held * CHUNKS * span, high)

    group = 5
    eye = jnp.eye(group, dtype=F32)
    act = jnp.einsum("gh,cut->gtchu", eye, actfock).reshape(group * active, 2 * group * active)
    act_high = lax.reduce_precision(act, 8, 7)
    act = jnp.stack([act_high, act - act_high]).astype(BF16)
    fit_rows = fitted.reshape(2, local_vir * active, local_fit)
    change = all_passes(fit_rows, flat, give, eps, row, act, n_vir)
    out = epilogue(eps, row, flat, change.reshape(CHUNKS * n_fit, own * active, lanes))
    out = out.reshape(local_vir, active // 2, 2, lanes).transpose(0, 2, 1, 3)
    return out.reshape(local_vir, 2, active * pairs).transpose(1, 0, 2)


def choose(mesh):
    def body(*args):
        n_fit, n_vir = mesh.shape["fit"], mesh.shape["vir"]
        fitted, vcouple, actfock, eps_vir, eps_act, pair_energy, source = args
        local_vir, active, local_fit = fitted.shape[1:]
        fits = (
            n_fit == 4
            and CHUNKS == 3
            and n_vir == 8
            and n_vir % 2 == 0
            and 2 * pair_energy.shape[0] == 128
            and n_vir * 16 == 128
            and local_vir % (CHUNKS * n_fit * 5) == 0
            and vcouple.shape[1] % local_vir == 0
            and active % 8 == 0
            and local_fit % (128 * HALVES) == 0
        )
        return per_device(*args) if fits else plain_device(*args)

    return body


def solution(mesh):
    return jax.shard_map(
        choose(mesh),
        mesh=mesh,
        in_specs=(
            P(None, "vir", None, "fit"),
            P(None, "fit", None),
            P(),
            P("vir"),
            P(),
            P(),
            P(None, "vir", None),
        ),
        out_specs=P(None, "vir", None),
        check_vma=False,
    )
```

```python
import jax
import jax.numpy as jnp
from jax import lax
from jax.experimental.layout import Layout, with_layout_constraint
from jax.experimental import pallas as pl
from jax.experimental.pallas import tpu as pltpu
from jax.sharding import PartitionSpec as P

PASSES = 3
CHUNKS = 3
SLOTS = 3
BF16 = jnp.bfloat16
F32 = jnp.float32
MESH = pl.DeviceIdType.MESH

def contract_first(left, right):
    return lax.dot_general(
        left, right, (((0,), (0,)), ((), ())), preferred_element_type=jnp.float32
    )


def plain_product(left, right):
    return jnp.dot(left, right, preferred_element_type=jnp.float32)


def active_coupling(values, actfock, active, pairs):
    highest = lax.Precision.HIGHEST
    local_vir = values.shape[1]
    grid = values.reshape(2, local_vir, active, pairs)
    act_real = jnp.einsum("aup,ut->atp", grid[0], actfock[0], precision=highest) - jnp.einsum(
        "aup,ut->atp", grid[1], actfock[1], precision=highest
    )
    act_imag = jnp.einsum("aup,ut->atp", grid[0], actfock[1], precision=highest) + jnp.einsum(
        "aup,ut->atp", grid[1], actfock[0], precision=highest
    )
    return jnp.stack([act_real, act_imag]).reshape(2, local_vir, actfock.shape[2] * pairs)


def plain_device(fitted, vcouple, actfock, eps_vir, eps_act, pair_energy, source):
    local_vir = fitted.shape[1]
    active = fitted.shape[2]
    local_fit = fitted.shape[3]
    pairs = pair_energy.shape[0]
    block_rows = vcouple.shape[1]
    width = local_vir * active
    fit_index = lax.axis_index("fit")
    denominator = (
        eps_vir[:, None, None] + eps_act[None, :, None] - pair_energy[None, None, :]
    ).reshape(local_vir, active * pairs)
    amplitude = source / denominator[None]
    fit_real = fitted[0].reshape(width, local_fit)
    fit_imag = fitted[1].reshape(width, local_fit)
    for pass_index in range(PASSES):
        rounded = amplitude.astype(jnp.bfloat16)
        flat_both = jnp.concatenate(
            [rounded[0].reshape(width, pairs), rounded[1].reshape(width, pairs)], axis=1
        )
        real_side = contract_first(fit_real, flat_both)
        imag_side = contract_first(fit_imag, flat_both)
        over_real = real_side[:, :pairs] + imag_side[:, pairs:]
        over_imag = real_side[:, pairs:] - imag_side[:, :pairs]
        intersection = lax.psum(jnp.concatenate([over_real, over_imag], axis=1), "vir").astype(
            jnp.bfloat16
        )
        real_out = plain_product(fit_real, intersection)
        imag_out = plain_product(fit_imag, intersection)
        sum_real = real_out[:, :pairs] - imag_out[:, pairs:]
        sum_imag = real_out[:, pairs:] + imag_out[:, :pairs]
        fitted_part = jnp.stack([sum_real, sum_imag]).reshape(2, local_vir, active * pairs)
        regrouped = lax.all_to_all(rounded, "vir", split_axis=2, concat_axis=1, tiled=True)
        window = lax.dynamic_slice_in_dim(regrouped, fit_index * block_rows, block_rows, 1)
        couple_real = contract_first(vcouple[0], window[0]) - contract_first(vcouple[1], window[1])
        couple_imag = contract_first(vcouple[1], window[0]) + contract_first(vcouple[0], window[1])
        coupled = jnp.stack([couple_real, couple_imag])
        returned = lax.all_to_all(coupled, "vir", split_axis=1, concat_axis=2, tiled=True)
        fitted_part = fitted_part + returned
        total = lax.psum(fitted_part, "fit")
        part_amplitude = amplitude
        active_term = active_coupling(amplitude, actfock, active, pairs)
        residual = source - denominator[None] * part_amplitude - active_term - total
        updated = part_amplitude + residual / denominator[None]
        amplitude = updated
    return amplitude


def turn(values, pairs):
    return jnp.concatenate([-values[..., pairs:], values[..., :pairs]], axis=-1)


def whole_vmem(count):
    return [pl.BlockSpec(memory_space=pltpu.VMEM)] * count


def mix(values, pairs):
    rows, lanes = values.shape
    even = lax.broadcasted_iota(jnp.int32, (rows, lanes), 0) % 2 == 0
    low = lax.broadcasted_iota(jnp.int32, (rows, lanes), 1) < pairs
    other = pltpu.roll(values, pairs, 1)
    up = pltpu.roll(other, rows - 1, 0)
    down = pltpu.roll(other, 1, 0)
    return jnp.where(even == low, values, jnp.where(even, up, down))


def epilogue_kernel(eps_ref, row_ref, source_ref, change_ref, out_ref, den):
    group, tile, lanes = change_ref.shape
    active = row_ref.shape[0]
    own = tile // active

    def one(j, carry):
        first = (pl.program_id(0) * group + j) * own
        for i in range(own):
            den[i * active : (i + 1) * active, :] = eps_ref[first + i] + row_ref[...]
        cut = pl.ds(pl.multiple_of(j * tile, 8), tile)
        start = mix(source_ref[cut, :], lanes // 2) / den[...]
        out_ref[cut, :] = mix(start + change_ref[j].astype(F32), lanes // 2)
        return carry

    lax.fori_loop(0, group, one, 0)


def epilogue(eps, row, source, change):
    pieces, tile, lanes = change.shape
    return pl.pallas_call(
        epilogue_kernel,
        grid=(pieces // CHUNKS,),
        in_specs=[
            pl.BlockSpec(memory_space=pltpu.SMEM),
            pl.BlockSpec(row.shape, lambda i: (0, 0)),
            pl.BlockSpec((CHUNKS * tile, lanes), lambda i: (i, 0)),
            pl.BlockSpec((CHUNKS, tile, lanes), lambda i: (i, 0, 0)),
        ],
        out_specs=pl.BlockSpec((CHUNKS * tile, lanes), lambda i: (i, 0)),
        out_shape=jax.ShapeDtypeStruct(source.shape, F32),
        scratch_shapes=[pltpu.VMEM((tile, lanes), F32)],
        compiler_params=pltpu.CompilerParams(vmem_limit_bytes=16 * 2**20),
        name="epilogue",
    )(eps, row, source, change)


def ring_of(vir, n):
    odd = vir % 2
    return (1 - odd) * (vir // 2) + odd * (n - 1 - vir // 2)


def vir_of(pos, n):
    pos = (pos + n) % n
    high = pos // (n // 2)
    return (1 - high) * (2 * pos) + high * (2 * (n - 1 - pos) + 1)


def choose_int(index, table):
    value = 0
    for key, entry in table.items():
        value = value + jnp.where(index == key, entry, 0)
    return value


def passes_kernel(
    n, f_ref, source_ref, give_ref, eps_ref, row_ref, act_ref, x_ref,
    buf, buf_sem, acc, part, parts, whole, inter, turned, ring, spread, rows, virtual,
    near, near_in, far, far_in, kept, amp, src, inverse, base, raw, den, couple, flipped,
    ring_send, ring_recv, part_send, part_recv, whole_send, whole_recv, init_sem,
    couple_send, couple_recv,
    near_send, near_recv, far_send, far_recv, gx_send, gx_recv, gc_send, gc_recv, gr_send, gr_recv,
):
    vir, fit = lax.axis_index("vir"), lax.axis_index("fit")
    chunks, n_fit, tile, lanes = x_ref.shape
    pairs = lanes // 2
    tiles = chunks * n_fit
    band = lanes // n
    depth = acc.shape[1]
    active = virtual.shape[1]
    span = spread.shape[0] // active
    half = n // 2
    pos = ring_of(vir, n)
    sides = ((vir_of(pos + 1, n), 1), (vir_of(pos - 1, n), -1))
    x, core = fit // 2, fit % 2
    beside = x * 2 + (1 - core)
    across = (1 - x) * 2 + core
    order = ((1 - x) * 2 + (1 - core), beside, across, fit)
    split = (chunks + 1) // 2
    group = act_ref.shape[1]

    def fetch(row_tile, slot):
        row = pl.multiple_of(row_tile * tile, 8)
        return pltpu.make_async_copy(
            f_ref.at[:, pl.ds(row, tile), :], buf.at[slot], buf_sem.at[slot]
        )

    def remote(src, dst, send, recv, axis, peer):
        return pltpu.make_async_remote_copy(
            src_ref=src, dst_ref=dst, send_sem=send, recv_sem=recv,
            device_id={axis: peer}, device_id_type=MESH,
        )

    def back_tile(k):
        value = 0
        for j in range(n_fit):
            value = value + jnp.where(k == j, order[j], 0)
        return value

    for i in range(SLOTS - 1):
        fetch(i, i).start()
    own = tile // active
    raw_copies = [
        pltpu.make_async_copy(
            source_ref.at[pl.ds(pl.multiple_of((c * n_fit + fit) * tile, 8), tile), :],
            src.at[c], init_sem.at[0, c],
        )
        for c in range(chunks)
    ]
    for copy in raw_copies:
        copy.start()
    bulk = pltpu.make_async_copy(source_ref, raw, init_sem.at[1, 0])
    bulk.start()
    own_couple = pltpu.make_async_copy(give_ref.at[fit], couple.at[fit], init_sem.at[1, 1])
    own_couple.start()

    barrier = pltpu.get_barrier_semaphore()
    for k in range(1, n):
        pl.semaphore_signal(barrier, inc=1, device_id={"vir": (vir + k) % n}, device_id_type=MESH)
    for k in range(1, n_fit):
        pl.semaphore_signal(
            barrier, inc=1, device_id={"fit": (fit + k) % n_fit}, device_id_type=MESH
        )

    def fill(first):
        for i in range(own):
            den[i * active : (i + 1) * active, :] = eps_ref[first + i] + row_ref[...]

    def begin(c, carry):
        fill((c * n_fit + fit) * own)
        source = mix(src[c], pairs)
        start = source / den[...]
        src[c] = source
        inverse[c] = 1.0 / den[...]
        amp[c] = start
        ring[0, vir, c] = start.astype(BF16)
        return carry

    for copy in raw_copies:
        copy.wait()
    lax.fori_loop(0, chunks, begin, 0)
    spread[...] = jnp.zeros_like(spread)
    pl.semaphore_wait(barrier, n + n_fit - 2)

    def sent_last(side, c):
        return (c < split) if side == 0 else (c >= split)

    def hop(parity, side, stage, c):
        to, sign = sides[side]
        owner = vir_of(pos - sign * (stage - 1), n)
        slot = ring.at[parity, owner, c]
        return remote(
            slot, slot, ring_send.at[side, stage - 1, c], ring_recv.at[side, stage - 1, c], "vir", to
        )

    def lay(parity, owner, c):
        spread[0:tile, :] = ring[parity, owner, c].astype(F32)
        top = pl.multiple_of((owner * chunks + c) * span, span)
        for t in range(active):
            rows[pl.ds(top, span), t * lanes : (t + 1) * lanes] = spread[
                pl.ds(t, span, stride=active), :
            ].astype(BF16)

    def landed(parity, side, stage, c):
        to, sign = sides[side]
        owner = vir_of(pos - sign * stage, n)
        slot = ring.at[parity, owner, c]
        remote(
            slot, slot, ring_send.at[side, stage - 1, c], ring_recv.at[side, stage - 1, c], "vir", to
        ).wait_recv()
        return owner

    def open_ring(parity, c):
        for side in range(2):
            hop(parity, side, 1, c).start()

    def relay(parity, stage, c):
        owners = []
        for side in range(2):
            owners.append(landed(parity, side, stage, c))

            @pl.when((stage < half - 1) | sent_last(side, c))
            def _():
                hop(parity, side, stage + 1, c).start()

        for owner in owners:
            lay(parity, owner, c)

    def part_copy(k):
        peer = (vir + k) % n
        return remote(
            part.at[peer], parts.at[vir], part_send.at[k - 1], part_recv.at[k - 1], "vir", peer
        )

    def part_landed(k):
        peer = (vir + n - k) % n
        remote(
            part.at[peer], parts.at[peer], part_send.at[k - 1], part_recv.at[k - 1], "vir", peer
        ).wait_recv()
        return peer

    def whole_copy(k):
        peer = (vir + k) % n
        return remote(
            whole.at[vir], whole.at[vir], whole_send.at[k - 1], whole_recv.at[k - 1], "vir", peer
        )

    def whole_landed(k):
        peer = (vir + n - k) % n
        remote(
            whole.at[peer], whole.at[peer], whole_send.at[k - 1], whole_recv.at[k - 1], "vir", peer
        ).wait_recv()

    def near_copy(c, k):
        return remote(
            near.at[c, k], near_in.at[c, k], near_send.at[c, k], near_recv.at[c, k], "fit", beside
        )

    def far_copy(c):
        return remote(far.at[c], far_in.at[c], far_send.at[c], far_recv.at[c], "fit", across)

    def gather_across(c, owner):
        slot = x_ref.at[c, owner]
        return remote(slot, slot, gx_send.at[c], gx_recv.at[c], "fit", across)

    def gather_beside(c, owner):
        slot = x_ref.at[c, owner]
        return remote(slot, slot, gc_send.at[c], gc_recv.at[c], "fit", beside)

    def gather_relay(c, owner):
        slot = x_ref.at[c, owner]
        return remote(slot, slot, gr_send.at[c], gr_recv.at[c], "fit", beside)

    def update(c, parity, final):
        far_copy(c).wait_recv()

        total = kept[c] + far_in[c].astype(F32)
        fresh = (base[c] - total) * inverse[c]
        amp[c] = fresh
        out = (fresh - jnp.where(final, src[c] * inverse[c], 0.0)).astype(BF16)
        x_ref[c, fit] = out
        gather_across(c, fit).start()
        gather_beside(c, fit).start()

        @pl.when(jnp.logical_not(final))
        def _():
            ring[parity, vir, c] = out
            open_ring(parity, c)

    def pass_on(c):
        gather_across(c, across).wait_recv()
        gather_relay(c, across).start()

    def gathered(c):
        gather_beside(c, beside).wait_recv()
        gather_relay(c, order[0]).wait_recv()

    def back_sends(c):
        for k in range(2):
            near_copy(c, k).wait_send()
        far_copy(c).wait_send()
        gather_across(c, fit).wait_send()
        gather_beside(c, fit).wait_send()
        gather_relay(c, across).wait_send()

    for c in range(chunks):
        open_ring(0, c)

    def couple_copy(k):
        peer = (fit + k) % n_fit
        return remote(
            give_ref.at[peer], couple.at[fit], couple_send.at[k - 1], couple_recv.at[k - 1], "fit", peer
        )

    def couple_landed(k):
        peer = (fit + n_fit - k) % n_fit
        remote(
            give_ref.at[peer], couple.at[peer], couple_send.at[k - 1], couple_recv.at[k - 1], "fit", peer
        ).wait_recv()

    for k in range(1, n_fit):
        couple_copy(k).start()

    def spread_start(i, carry):
        fill(i * own)
        source = raw[pl.ds(pl.multiple_of(i * tile, 8), tile), :]
        x_ref[i // n_fit, lax.rem(i, n_fit)] = (mix(source, pairs) / den[...]).astype(BF16)
        return carry

    bulk.wait()
    lax.fori_loop(0, tiles, spread_start, 0)

    def active_base(c, carry):
        value = amp[c]
        cuts = [value[g : g + group] for g in range(0, tile, group)]
        both = jnp.concatenate(
            [
                jnp.concatenate(cuts, axis=1),
                jnp.concatenate([turn(cut, pairs) for cut in cuts], axis=1),
            ],
            axis=0,
        )
        high = both.astype(BF16)
        low = (both - high.astype(F32)).astype(BF16)
        act = (
            plain_product(act_ref[0], high)
            + plain_product(act_ref[0], low)
            + plain_product(act_ref[1], high)
        )
        for g in range(tile // group):
            cut = slice(g * group, (g + 1) * group)
            base[c, cut, :] = src[c, cut, :] - act[:, g * lanes : (g + 1) * lanes]
        return carry

    contract = (((0,), (0,)), ((), ()))
    last_chunk = chunks - 1

    def one_pass(p, carry):
        parity = lax.rem(p, 2)
        later = p > 0
        acc[...] = jnp.zeros_like(acc)

        def contract_step(i, carry):
            ahead = i + SLOTS - 1
            inside = ahead < tiles
            target = jnp.where(inside, ahead, back_tile(ahead - tiles))
            fetch(target, lax.rem(ahead, SLOTS)).start()
            c = i // n_fit
            j = lax.rem(i, n_fit)

            @pl.when(later & (j == 0))
            def _():
                gathered(c)

            slot = lax.rem(i, SLOTS)
            fetch(i, slot).wait()
            values = x_ref[c, j]
            acc[...] += lax.dot_general(
                values, buf[slot, 0], contract, preferred_element_type=F32
            ) + lax.dot_general(
                -turn(values, pairs), buf[slot, 1], contract, preferred_element_type=F32
            )

            @pl.when(later & (i == 2))
            def _():
                update(last_chunk, parity, False)

            @pl.when(later & ((i == 1) | (i == 5)))
            def _():
                pass_on(jnp.where(i == 1, last_chunk - 1, last_chunk))

            code = jnp.where(later, choose_int(i, LATER_RELAYS), choose_int(i, FIRST_RELAYS))

            @pl.when(code > 0)
            def _():
                relay(parity, code // 8, lax.rem(code, 8))

            return carry

        lax.fori_loop(0, tiles, contract_step, 0)

        for k in range(n):
            part[k] = acc[k * band : (k + 1) * band, :].astype(BF16)
        for k in range(1, n):
            part_copy(k).start()

        @pl.when(later)
        def _():
            for c in range(chunks):
                back_sends(c)

        for c in range(chunks):
            lay(parity, vir, c)
        lax.fori_loop(0, chunks, active_base, 0)

        @pl.when(jnp.logical_not(later))
        def _():
            own_couple.wait()
            for k in range(1, n_fit):
                couple_landed(k)
            deep = couple.shape[2]
            for side in range(2):
                for j in range(n_fit):
                    flipped[side, :, j * deep : (j + 1) * deep] = (
                        couple[j, side].astype(F32).T.astype(BF16)
                    )

        total = acc[pl.ds(pl.multiple_of(vir * band, band), band), :]
        for k in range(1, n):
            total = total + parts[part_landed(k)].astype(F32)
        whole[vir] = total.astype(BF16)
        for k in range(1, n):
            whole_copy(k).start()
        for c in range(chunks):
            lay(parity, landed(parity, 0 if c < split else 1, half, c), c)
        heights = virtual.shape[0]
        padded = -(-heights // 16) * 16

        for t in range(0, active, 2):
            left = rows[:, t * lanes : (t + 1) * lanes]
            right = rows[:, (t + 1) * lanes : (t + 2) * lanes]
            plain = jnp.concatenate([left, right], axis=1)
            other = jnp.concatenate([turn(left, pairs), turn(right, pairs)], axis=1)
            value = plain_product(flipped[0, :padded], plain) + plain_product(
                flipped[1, :padded], other
            )
            virtual[:, t, :] = value[:heights, :lanes]
            virtual[:, t + 1, :] = value[:heights, lanes:]

        for c in range(chunks):
            for side in range(2):
                for stage in range(1, half + 1):
                    if stage < half or sent_last(side, c):
                        hop(parity, side, stage, c).wait_send()
        for k in range(1, n):
            whole_landed(k)
        block = depth
        for width in (512, 384, 256, 128):
            if depth % width == 0:
                block = width
                break
        for q in range(0, depth, block):
            cols = whole[:, :, q : q + block].reshape(lanes, block).astype(F32).T
            inter[q : q + block, :] = cols.astype(BF16)
            turned[q : q + block, :] = turn(cols, pairs).astype(BF16)
        for k in range(1, n):
            part_copy(k).wait_send()
            whole_copy(k).wait_send()

        final = p == PASSES - 1

        def back_chunk(c, carry):
            for k in range(n_fit):
                i = c * n_fit + k
                ahead = i + SLOTS - 1
                inside = ahead < tiles
                after = ahead - tiles
                target = jnp.where(
                    inside, (ahead // n_fit) * n_fit + order[(k + SLOTS - 1) % n_fit], after
                )

                @pl.when(inside | jnp.logical_not(final))
                def _():
                    fetch(target, lax.rem(ahead, SLOTS)).start()

                slot = lax.rem(i, SLOTS)
                where = c * n_fit + order[k]
                fetch(where, slot).wait()
                value = (
                    plain_product(buf[slot, 0], inter[...])
                    + plain_product(buf[slot, 1], turned[...])
                    + virtual[pl.ds(where * own, own)].reshape(tile, lanes)
                )
                if k < 2:
                    near[c, k] = value.astype(BF16)
                    near_copy(c, k).start()
                elif k == 2:
                    near_copy(c, 0).wait_recv()
                    far[c] = (value + near_in[c, 0].astype(F32)).astype(BF16)
                    far_copy(c).start()
                else:
                    near_copy(c, 1).wait_recv()
                    kept[c] = value + near_in[c, 1].astype(F32)
                if k == 0:

                    @pl.when(c >= 2)
                    def _():
                        pass_on(c - 2)

                    @pl.when((c >= 2) & jnp.logical_not(final))
                    def _():
                        relay(1 - parity, 1, c - 2)

                if k == 1:

                    @pl.when(c >= 1)
                    def _():
                        update(c - 1, 1 - parity, final)

                if k == 3:

                    @pl.when((c >= 2) & jnp.logical_not(final))
                    def _():
                        relay(1 - parity, 2, c - 2)

            return carry

        lax.fori_loop(0, chunks, back_chunk, 0)
        return carry

    lax.fori_loop(0, PASSES, one_pass, 0)
    pass_on(last_chunk - 1)
    update(last_chunk, 0, True)
    pass_on(last_chunk)
    for c in range(chunks):
        gathered(c)
        back_sends(c)
    for k in range(1, n_fit):
        couple_copy(k).wait_send()


FIRST_RELAYS = {1: 8, 2: 9, 3: 10, 5: 16, 6: 17, 7: 18, 9: 24, 10: 25, 11: 26}
LATER_RELAYS = {0: 9, 3: 24, 4: 17, 6: 10, 7: 25, 8: 18, 10: 26}


def all_passes(fit_rows, source, give, eps, row, act, n):
    depth = fit_rows.shape[2]
    active, lanes = row.shape
    n_fit, chunks = give.shape[0], CHUNKS
    local_vir = eps.shape[0]
    tile = local_vir // (chunks * n_fit) * active
    wide = n_fit * give.shape[2]
    span = wide // (chunks * n)
    half = n // 2
    dma = pltpu.SemaphoreType.DMA
    band = pltpu.VMEM((n, lanes // n, depth), BF16)
    each = pltpu.VMEM((chunks, tile, lanes), BF16)
    twice = pltpu.VMEM((chunks, 2, tile, lanes), BF16)
    state = pltpu.VMEM((chunks, tile, lanes), F32)
    any_space = pl.BlockSpec(memory_space=pl.ANY)
    return pl.pallas_call(
        lambda *refs: passes_kernel(n, *refs),
        in_specs=[any_space, any_space]
        + whole_vmem(1)
        + [pl.BlockSpec(memory_space=pltpu.SMEM)]
        + whole_vmem(2),
        out_specs=pl.BlockSpec(memory_space=pltpu.VMEM),
        out_shape=jax.ShapeDtypeStruct((chunks, n_fit, tile, lanes), BF16),
        scratch_shapes=[
            pltpu.VMEM((SLOTS, 2, tile, depth), BF16),
            dma((SLOTS,)),
            pltpu.VMEM((lanes, depth), F32),
            band,
            band,
            band,
            pltpu.VMEM((depth, lanes), BF16),
            pltpu.VMEM((depth, lanes), BF16),
            pltpu.VMEM((2, n, chunks, tile, lanes), BF16),
            pltpu.VMEM((span * active, lanes), F32),
            pltpu.VMEM((wide, active * lanes), BF16),
            pltpu.VMEM((local_vir, active, lanes), F32),
            twice,
            twice,
            each,
            each,
            state,
            state,
            state,
            state,
            state,
            pltpu.VMEM((local_vir * active, lanes), F32),
            pltpu.VMEM((tile, lanes), F32),
            pltpu.VMEM(give.shape, BF16),
            pltpu.VMEM((2, give.shape[3], wide), BF16),
            dma((2, half, chunks)),
            dma((2, half, chunks)),
        ]
        + [dma((n - 1,))] * 4
        + [dma((2, chunks))]
        + [dma((n_fit - 1,))] * 2
        + [dma((chunks, 2))] * 2
        + [dma((chunks,))] * 8,
        compiler_params=pltpu.CompilerParams(
            collective_id=0, has_side_effects=True, vmem_limit_bytes=60 * 2**20
        ),
        name="passes",
    )(fit_rows, source, give, eps, row, act)


def per_device(fitted, vcouple, actfock, eps_vir, eps_act, pair_energy, source):
    n_fit, n_vir = lax.axis_size("fit"), lax.axis_size("vir")
    vir_index = lax.axis_index("vir")
    local_vir, active, local_fit = fitted.shape[1:]
    block_rows = vcouple.shape[1]
    pairs = pair_energy.shape[0]
    lanes = 2 * pairs
    own = local_vir // (CHUNKS * n_fit)
    span = -(-own // 16) * 16
    held = block_rows // local_vir
    high = -(-local_vir // 128) * 128

    row = eps_act[:, None] - pair_energy[None, :]
    row = jnp.concatenate([row, row], axis=1)
    flat = source.reshape(2, local_vir, active // 2, lanes)
    flat = with_layout_constraint(flat, Layout(major_to_minor=(1, 2, 0, 3)))
    flat = flat.transpose(1, 2, 0, 3).reshape(local_vir * active, lanes)

    give = lax.dynamic_slice_in_dim(vcouple, vir_index * local_vir, local_vir, 2)
    give = give.reshape(2, held, CHUNKS, n_fit, own, local_vir).transpose(3, 0, 1, 2, 4, 5)
    give = jnp.pad(give, ((0, 0),) * 4 + ((0, span - own), (0, high - local_vir)))
    give = give.reshape(n_fit, 2, held * CHUNKS * span, high)

    group = 5
    eye = jnp.eye(group, dtype=F32)
    act = jnp.einsum("gh,cut->gtchu", eye, actfock).reshape(group * active, 2 * group * active)
    act_high = lax.reduce_precision(act, 8, 7)
    act = jnp.stack([act_high, act - act_high]).astype(BF16)
    fit_rows = fitted.reshape(2, local_vir * active, local_fit)
    change = all_passes(fit_rows, flat, give, eps_vir, row, act, n_vir)
    out = epilogue(eps_vir, row, flat, change.reshape(CHUNKS * n_fit, own * active, lanes))
    out = out.reshape(local_vir, active // 2, 2, lanes).transpose(0, 2, 1, 3)
    return out.reshape(local_vir, 2, active * pairs).transpose(1, 0, 2)


def choose(mesh):
    def body(*args):
        n_fit, n_vir = mesh.shape["fit"], mesh.shape["vir"]
        fitted, vcouple, actfock, eps_vir, eps_act, pair_energy, source = args
        local_vir, active, local_fit = fitted.shape[1:]
        fits = (
            n_fit == 4
            and CHUNKS == 3
            and n_vir == 8
            and n_vir % 2 == 0
            and 2 * pair_energy.shape[0] == 128
            and n_vir * 16 == 128
            and local_vir % (CHUNKS * n_fit * 5) == 0
            and vcouple.shape[1] % local_vir == 0
            and active % 8 == 0
            and local_fit % 128 == 0
        )
        return per_device(*args) if fits else plain_device(*args)

    return body


def solution(mesh):
    return jax.shard_map(
        choose(mesh),
        mesh=mesh,
        in_specs=(
            P(None, "vir", None, "fit"),
            P(None, "fit", None),
            P(),
            P("vir"),
            P(),
            P(),
            P(None, "vir", None),
        ),
        out_specs=P(None, "vir", None),
        check_vma=False,
    )
```

```python
import jax
import jax.numpy as jnp
from jax import lax
from jax.experimental.layout import Layout, with_layout_constraint
from jax.experimental import pallas as pl
from jax.experimental.pallas import tpu as pltpu
from jax.sharding import PartitionSpec as P

PASSES = 3
CHUNKS = 3
SLOTS = 3
BF16 = jnp.bfloat16
F32 = jnp.float32
MESH = pl.DeviceIdType.MESH

def contract_first(left, right):
    return lax.dot_general(
        left, right, (((0,), (0,)), ((), ())), preferred_element_type=jnp.float32
    )


def plain_product(left, right):
    return jnp.dot(left, right, preferred_element_type=jnp.float32)


def active_coupling(values, actfock, active, pairs):
    highest = lax.Precision.HIGHEST
    local_vir = values.shape[1]
    grid = values.reshape(2, local_vir, active, pairs)
    act_real = jnp.einsum("aup,ut->atp", grid[0], actfock[0], precision=highest) - jnp.einsum(
        "aup,ut->atp", grid[1], actfock[1], precision=highest
    )
    act_imag = jnp.einsum("aup,ut->atp", grid[0], actfock[1], precision=highest) + jnp.einsum(
        "aup,ut->atp", grid[1], actfock[0], precision=highest
    )
    return jnp.stack([act_real, act_imag]).reshape(2, local_vir, actfock.shape[2] * pairs)


def plain_device(fitted, vcouple, actfock, eps_vir, eps_act, pair_energy, source):
    local_vir = fitted.shape[1]
    active = fitted.shape[2]
    local_fit = fitted.shape[3]
    pairs = pair_energy.shape[0]
    block_rows = vcouple.shape[1]
    width = local_vir * active
    fit_index = lax.axis_index("fit")
    denominator = (
        eps_vir[:, None, None] + eps_act[None, :, None] - pair_energy[None, None, :]
    ).reshape(local_vir, active * pairs)
    amplitude = source / denominator[None]
    fit_real = fitted[0].reshape(width, local_fit)
    fit_imag = fitted[1].reshape(width, local_fit)
    for pass_index in range(PASSES):
        rounded = amplitude.astype(jnp.bfloat16)
        flat_both = jnp.concatenate(
            [rounded[0].reshape(width, pairs), rounded[1].reshape(width, pairs)], axis=1
        )
        real_side = contract_first(fit_real, flat_both)
        imag_side = contract_first(fit_imag, flat_both)
        over_real = real_side[:, :pairs] + imag_side[:, pairs:]
        over_imag = real_side[:, pairs:] - imag_side[:, :pairs]
        intersection = lax.psum(jnp.concatenate([over_real, over_imag], axis=1), "vir").astype(
            jnp.bfloat16
        )
        real_out = plain_product(fit_real, intersection)
        imag_out = plain_product(fit_imag, intersection)
        sum_real = real_out[:, :pairs] - imag_out[:, pairs:]
        sum_imag = real_out[:, pairs:] + imag_out[:, :pairs]
        fitted_part = jnp.stack([sum_real, sum_imag]).reshape(2, local_vir, active * pairs)
        regrouped = lax.all_to_all(rounded, "vir", split_axis=2, concat_axis=1, tiled=True)
        window = lax.dynamic_slice_in_dim(regrouped, fit_index * block_rows, block_rows, 1)
        couple_real = contract_first(vcouple[0], window[0]) - contract_first(vcouple[1], window[1])
        couple_imag = contract_first(vcouple[1], window[0]) + contract_first(vcouple[0], window[1])
        coupled = jnp.stack([couple_real, couple_imag])
        returned = lax.all_to_all(coupled, "vir", split_axis=1, concat_axis=2, tiled=True)
        fitted_part = fitted_part + returned
        total = lax.psum(fitted_part, "fit")
        part_amplitude = amplitude
        active_term = active_coupling(amplitude, actfock, active, pairs)
        residual = source - denominator[None] * part_amplitude - active_term - total
        updated = part_amplitude + residual / denominator[None]
        amplitude = updated
    return amplitude


def turn(values, pairs):
    return jnp.concatenate([-values[..., pairs:], values[..., :pairs]], axis=-1)


def whole_vmem(count):
    return [pl.BlockSpec(memory_space=pltpu.VMEM)] * count


def mix(values, pairs):
    rows, lanes = values.shape
    even = lax.broadcasted_iota(jnp.int32, (rows, lanes), 0) % 2 == 0
    low = lax.broadcasted_iota(jnp.int32, (rows, lanes), 1) < pairs
    other = pltpu.roll(values, pairs, 1)
    up = pltpu.roll(other, rows - 1, 0)
    down = pltpu.roll(other, 1, 0)
    return jnp.where(even == low, values, jnp.where(even, up, down))


def epilogue_kernel(eps_ref, row_ref, source_ref, change_ref, out_ref, den):
    group, tile, lanes = change_ref.shape
    active = row_ref.shape[0]
    own = tile // active

    def one(j, carry):
        first = (pl.program_id(0) * group + j) * own
        for i in range(own):
            den[i * active : (i + 1) * active, :] = eps_ref[first + i] + row_ref[...]
        cut = pl.ds(pl.multiple_of(j * tile, 8), tile)
        start = mix(source_ref[cut, :], lanes // 2) / den[...]
        out_ref[cut, :] = mix(start + change_ref[j].astype(F32), lanes // 2)
        return carry

    lax.fori_loop(0, group, one, 0)


def epilogue(eps, row, source, change):
    pieces, tile, lanes = change.shape
    return pl.pallas_call(
        epilogue_kernel,
        grid=(pieces // CHUNKS,),
        in_specs=[
            pl.BlockSpec(memory_space=pltpu.SMEM),
            pl.BlockSpec(row.shape, lambda i: (0, 0)),
            pl.BlockSpec((CHUNKS * tile, lanes), lambda i: (i, 0)),
            pl.BlockSpec((CHUNKS, tile, lanes), lambda i: (i, 0, 0)),
        ],
        out_specs=pl.BlockSpec((CHUNKS * tile, lanes), lambda i: (i, 0)),
        out_shape=jax.ShapeDtypeStruct(source.shape, F32),
        scratch_shapes=[pltpu.VMEM((tile, lanes), F32)],
        compiler_params=pltpu.CompilerParams(vmem_limit_bytes=16 * 2**20),
        name="epilogue",
    )(eps, row, source, change)


def ring_of(vir, n):
    odd = vir % 2
    return (1 - odd) * (vir // 2) + odd * (n - 1 - vir // 2)


def vir_of(pos, n):
    pos = (pos + n) % n
    high = pos // (n // 2)
    return (1 - high) * (2 * pos) + high * (2 * (n - 1 - pos) + 1)


def choose_int(index, table):
    value = 0
    for key, entry in table.items():
        value = value + jnp.where(index == key, entry, 0)
    return value


def passes_kernel(
    n, f_ref, source_ref, give_ref, eps_ref, row_ref, act_ref, x_ref,
    buf, buf_sem, acc, part, side_in, line, line_in, whole, inter, turned, ring, spread, rows, virtual,
    near, near_in, far, far_in, kept, amp, src, inverse, base, raw, den, couple, flipped,
    ring_send, ring_recv, side_send, side_recv, line_send, line_recv, whole_send, whole_recv,
    pass_send, pass_recv, init_sem,
    couple_send, couple_recv,
    near_send, near_recv, far_send, far_recv, gx_send, gx_recv, gc_send, gc_recv, gr_send, gr_recv,
):
    vir, fit = lax.axis_index("vir"), lax.axis_index("fit")
    chunks, n_fit, tile, lanes = x_ref.shape
    pairs = lanes // 2
    tiles = chunks * n_fit
    band = lanes // n
    depth = acc.shape[1]
    line_size = n // 2
    level, lane_side = vir // 2, vir % 2
    partner = vir + 1 - 2 * lane_side
    active = virtual.shape[1]
    span = spread.shape[0] // active
    half = n // 2
    pos = ring_of(vir, n)
    sides = ((vir_of(pos + 1, n), 1), (vir_of(pos - 1, n), -1))
    x, core = fit // 2, fit % 2
    beside = x * 2 + (1 - core)
    across = (1 - x) * 2 + core
    order = ((1 - x) * 2 + (1 - core), beside, across, fit)
    split = (chunks + 1) // 2
    group = act_ref.shape[1]

    def fetch(row_tile, slot):
        row = pl.multiple_of(row_tile * tile, 8)
        return pltpu.make_async_copy(
            f_ref.at[:, pl.ds(row, tile), :], buf.at[slot], buf_sem.at[slot]
        )

    def remote(src, dst, send, recv, axis, peer):
        return pltpu.make_async_remote_copy(
            src_ref=src, dst_ref=dst, send_sem=send, recv_sem=recv,
            device_id={axis: peer}, device_id_type=MESH,
        )

    def back_tile(k):
        value = 0
        for j in range(n_fit):
            value = value + jnp.where(k == j, order[j], 0)
        return value

    for i in range(SLOTS - 1):
        fetch(i, i).start()
    own = tile // active
    raw_copies = [
        pltpu.make_async_copy(
            source_ref.at[pl.ds(pl.multiple_of((c * n_fit + fit) * tile, 8), tile), :],
            src.at[c], init_sem.at[0, c],
        )
        for c in range(chunks)
    ]
    for copy in raw_copies:
        copy.start()
    bulk = pltpu.make_async_copy(source_ref, raw, init_sem.at[1, 0])
    bulk.start()
    own_couple = pltpu.make_async_copy(give_ref.at[fit], couple.at[fit], init_sem.at[1, 1])
    own_couple.start()

    barrier = pltpu.get_barrier_semaphore()
    for k in range(1, n):
        pl.semaphore_signal(barrier, inc=1, device_id={"vir": (vir + k) % n}, device_id_type=MESH)
    for k in range(1, n_fit):
        pl.semaphore_signal(
            barrier, inc=1, device_id={"fit": (fit + k) % n_fit}, device_id_type=MESH
        )

    def fill(first):
        for i in range(own):
            den[i * active : (i + 1) * active, :] = eps_ref[first + i] + row_ref[...]

    def begin(c, carry):
        fill((c * n_fit + fit) * own)
        source = mix(src[c], pairs)
        start = source / den[...]
        src[c] = source
        inverse[c] = 1.0 / den[...]
        amp[c] = start
        ring[0, vir, c] = start.astype(BF16)
        return carry

    for copy in raw_copies:
        copy.wait()
    lax.fori_loop(0, chunks, begin, 0)
    spread[...] = jnp.zeros_like(spread)
    pl.semaphore_wait(barrier, n + n_fit - 2)

    def sent_last(side, c):
        return (c < split) if side == 0 else (c >= split)

    def hop(parity, side, stage, c):
        to, sign = sides[side]
        owner = vir_of(pos - sign * (stage - 1), n)
        slot = ring.at[parity, owner, c]
        return remote(
            slot, slot, ring_send.at[side, stage - 1, c], ring_recv.at[side, stage - 1, c], "vir", to
        )

    def lay(parity, owner, c):
        spread[0:tile, :] = ring[parity, owner, c].astype(F32)
        top = pl.multiple_of((owner * chunks + c) * span, span)
        for t in range(active):
            rows[pl.ds(top, span), t * lanes : (t + 1) * lanes] = spread[
                pl.ds(t, span, stride=active), :
            ].astype(BF16)

    def landed(parity, side, stage, c):
        to, sign = sides[side]
        owner = vir_of(pos - sign * stage, n)
        slot = ring.at[parity, owner, c]
        remote(
            slot, slot, ring_send.at[side, stage - 1, c], ring_recv.at[side, stage - 1, c], "vir", to
        ).wait_recv()
        return owner

    def open_ring(parity, c):
        for side in range(2):
            hop(parity, side, 1, c).start()

    def relay(parity, stage, c):
        owners = []
        for side in range(2):
            owners.append(landed(parity, side, stage, c))

            @pl.when((stage < half - 1) | sent_last(side, c))
            def _():
                hop(parity, side, stage + 1, c).start()

        for owner in owners:
            lay(parity, owner, c)

    def side_copy():
        return remote(
            part.at[1 - lane_side], side_in, side_send.at[0], side_recv.at[0], "vir", partner
        )

    def line_copy(k):
        to = (level + k) % line_size
        return remote(
            line.at[to], line_in.at[level], line_send.at[k - 1], line_recv.at[k - 1],
            "vir", 2 * to + lane_side,
        )

    def line_landed(k):
        source = (level + line_size - k) % line_size
        remote(
            line.at[source], line_in.at[source], line_send.at[k - 1], line_recv.at[k - 1],
            "vir", 2 * source + lane_side,
        ).wait_recv()
        return source

    def whole_copy(k):
        slot = whole.at[vir]
        peer = partner if k == 0 else 2 * ((level + k) % line_size) + lane_side
        return remote(slot, slot, whole_send.at[k], whole_recv.at[k], "vir", peer)

    def whole_landed(k):
        peer = partner if k == 0 else 2 * ((level + line_size - k) % line_size) + lane_side
        slot = whole.at[peer]
        remote(slot, slot, whole_send.at[k], whole_recv.at[k], "vir", peer).wait_recv()

    def pass_copy(k, side):
        slot = whole.at[2 * ((level + line_size - k) % line_size) + side]
        return remote(slot, slot, pass_send.at[k - 1], pass_recv.at[k - 1], "vir", partner)

    def own_band(index):
        return pl.ds(pl.multiple_of((2 * index + lane_side) * band, band), band)

    def near_copy(c, k):
        return remote(
            near.at[c, k], near_in.at[c, k], near_send.at[c, k], near_recv.at[c, k], "fit", beside
        )

    def far_copy(c):
        return remote(far.at[c], far_in.at[c], far_send.at[c], far_recv.at[c], "fit", across)

    def gather_across(c, owner):
        slot = x_ref.at[c, owner]
        return remote(slot, slot, gx_send.at[c], gx_recv.at[c], "fit", across)

    def gather_beside(c, owner):
        slot = x_ref.at[c, owner]
        return remote(slot, slot, gc_send.at[c], gc_recv.at[c], "fit", beside)

    def gather_relay(c, owner):
        slot = x_ref.at[c, owner]
        return remote(slot, slot, gr_send.at[c], gr_recv.at[c], "fit", beside)

    def update(c, parity, final):
        far_copy(c).wait_recv()

        total = kept[c] + far_in[c].astype(F32)
        fresh = (base[c] - total) * inverse[c]
        amp[c] = fresh
        out = (fresh - jnp.where(final, src[c] * inverse[c], 0.0)).astype(BF16)
        x_ref[c, fit] = out
        gather_across(c, fit).start()
        gather_beside(c, fit).start()

        @pl.when(jnp.logical_not(final))
        def _():
            ring[parity, vir, c] = out
            open_ring(parity, c)

    def pass_on(c):
        gather_across(c, across).wait_recv()
        gather_relay(c, across).start()

    def gathered(c):
        gather_beside(c, beside).wait_recv()
        gather_relay(c, order[0]).wait_recv()

    def back_sends(c):
        for k in range(2):
            near_copy(c, k).wait_send()
        far_copy(c).wait_send()
        gather_across(c, fit).wait_send()
        gather_beside(c, fit).wait_send()
        gather_relay(c, across).wait_send()

    for c in range(chunks):
        open_ring(0, c)

    def couple_copy(k):
        peer = (fit + k) % n_fit
        return remote(
            give_ref.at[peer], couple.at[fit], couple_send.at[k - 1], couple_recv.at[k - 1], "fit", peer
        )

    def couple_landed(k):
        peer = (fit + n_fit - k) % n_fit
        remote(
            give_ref.at[peer], couple.at[peer], couple_send.at[k - 1], couple_recv.at[k - 1], "fit", peer
        ).wait_recv()

    for k in range(1, n_fit):
        couple_copy(k).start()

    def spread_start(i, carry):
        fill(i * own)
        source = raw[pl.ds(pl.multiple_of(i * tile, 8), tile), :]
        x_ref[i // n_fit, lax.rem(i, n_fit)] = (mix(source, pairs) / den[...]).astype(BF16)
        return carry

    bulk.wait()
    lax.fori_loop(0, tiles, spread_start, 0)

    def active_base(c, carry):
        value = amp[c]
        cuts = [value[g : g + group] for g in range(0, tile, group)]
        both = jnp.concatenate(
            [
                jnp.concatenate(cuts, axis=1),
                jnp.concatenate([turn(cut, pairs) for cut in cuts], axis=1),
            ],
            axis=0,
        )
        high = both.astype(BF16)
        low = (both - high.astype(F32)).astype(BF16)
        act = (
            plain_product(act_ref[0], high)
            + plain_product(act_ref[0], low)
            + plain_product(act_ref[1], high)
        )
        for g in range(tile // group):
            cut = slice(g * group, (g + 1) * group)
            base[c, cut, :] = src[c, cut, :] - act[:, g * lanes : (g + 1) * lanes]
        return carry

    contract = (((0,), (0,)), ((), ()))
    last_chunk = chunks - 1

    def one_pass(p, carry):
        parity = lax.rem(p, 2)
        later = p > 0
        acc[...] = jnp.zeros_like(acc)

        def contract_step(i, carry):
            ahead = i + SLOTS - 1
            inside = ahead < tiles
            target = jnp.where(inside, ahead, back_tile(ahead - tiles))
            fetch(target, lax.rem(ahead, SLOTS)).start()
            c = i // n_fit
            j = lax.rem(i, n_fit)

            @pl.when(later & (j == 0))
            def _():
                gathered(c)

            slot = lax.rem(i, SLOTS)
            fetch(i, slot).wait()
            values = x_ref[c, j]
            acc[...] += lax.dot_general(
                values, buf[slot, 0], contract, preferred_element_type=F32
            ) + lax.dot_general(
                -turn(values, pairs), buf[slot, 1], contract, preferred_element_type=F32
            )

            @pl.when(later & (i == 2))
            def _():
                update(last_chunk, parity, False)

            @pl.when(later & ((i == 1) | (i == 5)))
            def _():
                pass_on(jnp.where(i == 1, last_chunk - 1, last_chunk))

            code = jnp.where(later, choose_int(i, LATER_RELAYS), choose_int(i, FIRST_RELAYS))

            @pl.when(code > 0)
            def _():
                relay(parity, code // 8, lax.rem(code, 8))

            return carry

        lax.fori_loop(0, tiles, contract_step, 0)

        for k in range(n):
            part[k % 2, k // 2] = acc[k * band : (k + 1) * band, :].astype(BF16)
        side_copy().start()

        @pl.when(later)
        def _():
            for c in range(chunks):
                back_sends(c)

        for c in range(chunks):
            lay(parity, vir, c)
        side_copy().wait_recv()
        for k in range(line_size):
            both = acc[own_band(k), :] + side_in[k].astype(F32)
            acc[own_band(k), :] = both
            line[k] = both.astype(BF16)
        for k in range(1, line_size):
            line_copy(k).start()
        lax.fori_loop(0, chunks, active_base, 0)

        @pl.when(jnp.logical_not(later))
        def _():
            own_couple.wait()
            for k in range(1, n_fit):
                couple_landed(k)
            deep = couple.shape[2]
            for side in range(2):
                for j in range(n_fit):
                    flipped[side, :, j * deep : (j + 1) * deep] = (
                        couple[j, side].astype(F32).T.astype(BF16)
                    )

        total = acc[own_band(level), :]
        for k in range(1, line_size):
            total = total + line_in[line_landed(k)].astype(F32)
        whole[vir] = total.astype(BF16)
        for k in range(line_size):
            whole_copy(k).start()
        for c in range(chunks):
            lay(parity, landed(parity, 0 if c < split else 1, half, c), c)
        for k in range(1, line_size):
            whole_landed(k)
            pass_copy(k, lane_side).start()
        heights = virtual.shape[0]
        padded = -(-heights // 16) * 16

        for t in range(0, active, 2):
            left = rows[:, t * lanes : (t + 1) * lanes]
            right = rows[:, (t + 1) * lanes : (t + 2) * lanes]
            plain = jnp.concatenate([left, right], axis=1)
            other = jnp.concatenate([turn(left, pairs), turn(right, pairs)], axis=1)
            value = plain_product(flipped[0, :padded], plain) + plain_product(
                flipped[1, :padded], other
            )
            virtual[:, t, :] = value[:heights, :lanes]
            virtual[:, t + 1, :] = value[:heights, lanes:]

        for c in range(chunks):
            for side in range(2):
                for stage in range(1, half + 1):
                    if stage < half or sent_last(side, c):
                        hop(parity, side, stage, c).wait_send()
        whole_landed(0)
        for k in range(1, line_size):
            pass_copy(k, 1 - lane_side).wait_recv()
        block = depth
        for width in (512, 384, 256, 128):
            if depth % width == 0:
                block = width
                break
        for q in range(0, depth, block):
            cols = whole[:, :, q : q + block].reshape(lanes, block).astype(F32).T
            inter[q : q + block, :] = cols.astype(BF16)
            turned[q : q + block, :] = turn(cols, pairs).astype(BF16)
        side_copy().wait_send()
        for k in range(1, line_size):
            line_copy(k).wait_send()
            pass_copy(k, lane_side).wait_send()
        for k in range(line_size):
            whole_copy(k).wait_send()

        final = p == PASSES - 1

        def back_chunk(c, carry):
            for k in range(n_fit):
                i = c * n_fit + k
                ahead = i + SLOTS - 1
                inside = ahead < tiles
                after = ahead - tiles
                target = jnp.where(
                    inside, (ahead // n_fit) * n_fit + order[(k + SLOTS - 1) % n_fit], after
                )

                @pl.when(inside | jnp.logical_not(final))
                def _():
                    fetch(target, lax.rem(ahead, SLOTS)).start()

                slot = lax.rem(i, SLOTS)
                where = c * n_fit + order[k]
                fetch(where, slot).wait()
                value = (
                    plain_product(buf[slot, 0], inter[...])
                    + plain_product(buf[slot, 1], turned[...])
                    + virtual[pl.ds(where * own, own)].reshape(tile, lanes)
                )
                if k < 2:
                    near[c, k] = value.astype(BF16)
                    near_copy(c, k).start()
                elif k == 2:
                    near_copy(c, 0).wait_recv()
                    far[c] = (value + near_in[c, 0].astype(F32)).astype(BF16)
                    far_copy(c).start()
                else:
                    near_copy(c, 1).wait_recv()
                    kept[c] = value + near_in[c, 1].astype(F32)
                if k == 0:

                    @pl.when(c >= 2)
                    def _():
                        pass_on(c - 2)

                    @pl.when((c >= 2) & jnp.logical_not(final))
                    def _():
                        relay(1 - parity, 1, c - 2)

                if k == 1:

                    @pl.when(c >= 1)
                    def _():
                        update(c - 1, 1 - parity, final)

                if k == 3:

                    @pl.when((c >= 2) & jnp.logical_not(final))
                    def _():
                        relay(1 - parity, 2, c - 2)

            return carry

        lax.fori_loop(0, chunks, back_chunk, 0)
        return carry

    lax.fori_loop(0, PASSES, one_pass, 0)
    pass_on(last_chunk - 1)
    update(last_chunk, 0, True)
    pass_on(last_chunk)
    for c in range(chunks):
        gathered(c)
        back_sends(c)
    for k in range(1, n_fit):
        couple_copy(k).wait_send()


FIRST_RELAYS = {2: 8, 4: 9, 5: 10, 6: 16, 7: 17, 8: 18, 9: 24, 10: 25, 11: 26}
LATER_RELAYS = {1: 9, 4: 24, 5: 17, 7: 10, 8: 25, 9: 18, 11: 26}


def all_passes(fit_rows, source, give, eps, row, act, n):
    depth = fit_rows.shape[2]
    active, lanes = row.shape
    n_fit, chunks = give.shape[0], CHUNKS
    local_vir = eps.shape[0]
    tile = local_vir // (chunks * n_fit) * active
    wide = n_fit * give.shape[2]
    span = wide // (chunks * n)
    half = n // 2
    dma = pltpu.SemaphoreType.DMA
    line = pltpu.VMEM((n // 2, lanes // n, depth), BF16)
    each = pltpu.VMEM((chunks, tile, lanes), BF16)
    twice = pltpu.VMEM((chunks, 2, tile, lanes), BF16)
    state = pltpu.VMEM((chunks, tile, lanes), F32)
    any_space = pl.BlockSpec(memory_space=pl.ANY)
    return pl.pallas_call(
        lambda *refs: passes_kernel(n, *refs),
        in_specs=[any_space, any_space]
        + whole_vmem(1)
        + [pl.BlockSpec(memory_space=pltpu.SMEM)]
        + whole_vmem(2),
        out_specs=pl.BlockSpec(memory_space=pltpu.VMEM),
        out_shape=jax.ShapeDtypeStruct((chunks, n_fit, tile, lanes), BF16),
        scratch_shapes=[
            pltpu.VMEM((SLOTS, 2, tile, depth), BF16),
            dma((SLOTS,)),
            pltpu.VMEM((lanes, depth), F32),
            pltpu.VMEM((2, n // 2, lanes // n, depth), BF16),
            line,
            line,
            line,
            pltpu.VMEM((n, lanes // n, depth), BF16),
            pltpu.VMEM((depth, lanes), BF16),
            pltpu.VMEM((depth, lanes), BF16),
            pltpu.VMEM((2, n, chunks, tile, lanes), BF16),
            pltpu.VMEM((span * active, lanes), F32),
            pltpu.VMEM((wide, active * lanes), BF16),
            pltpu.VMEM((local_vir, active, lanes), F32),
            twice,
            twice,
            each,
            each,
            state,
            state,
            state,
            state,
            state,
            pltpu.VMEM((local_vir * active, lanes), F32),
            pltpu.VMEM((tile, lanes), F32),
            pltpu.VMEM(give.shape, BF16),
            pltpu.VMEM((2, give.shape[3], wide), BF16),
            dma((2, half, chunks)),
            dma((2, half, chunks)),
        ]
        + [dma((1,))] * 2
        + [dma((n // 2 - 1,))] * 2
        + [dma((n // 2,))] * 2
        + [dma((n // 2 - 1,))] * 2
        + [dma((2, chunks))]
        + [dma((n_fit - 1,))] * 2
        + [dma((chunks, 2))] * 2
        + [dma((chunks,))] * 8,
        compiler_params=pltpu.CompilerParams(
            collective_id=0, has_side_effects=True, vmem_limit_bytes=60 * 2**20
        ),
        name="passes",
    )(fit_rows, source, give, eps, row, act)


def per_device(fitted, vcouple, actfock, eps_vir, eps_act, pair_energy, source):
    n_fit, n_vir = lax.axis_size("fit"), lax.axis_size("vir")
    vir_index = lax.axis_index("vir")
    local_vir, active, local_fit = fitted.shape[1:]
    block_rows = vcouple.shape[1]
    pairs = pair_energy.shape[0]
    lanes = 2 * pairs
    own = local_vir // (CHUNKS * n_fit)
    span = -(-own // 16) * 16
    held = block_rows // local_vir
    high = -(-local_vir // 128) * 128

    row = eps_act[:, None] - pair_energy[None, :]
    row = jnp.concatenate([row, row], axis=1)
    flat = source.reshape(2, local_vir, active // 2, lanes)
    flat = with_layout_constraint(flat, Layout(major_to_minor=(1, 2, 0, 3)))
    flat = flat.transpose(1, 2, 0, 3).reshape(local_vir * active, lanes)

    give = lax.dynamic_slice_in_dim(vcouple, vir_index * local_vir, local_vir, 2)
    give = give.reshape(2, held, CHUNKS, n_fit, own, local_vir).transpose(3, 0, 1, 2, 4, 5)
    give = jnp.pad(give, ((0, 0),) * 4 + ((0, span - own), (0, high - local_vir)))
    give = give.reshape(n_fit, 2, held * CHUNKS * span, high)

    group = 5
    eye = jnp.eye(group, dtype=F32)
    act = jnp.einsum("gh,cut->gtchu", eye, actfock).reshape(group * active, 2 * group * active)
    act_high = lax.reduce_precision(act, 8, 7)
    act = jnp.stack([act_high, act - act_high]).astype(BF16)
    fit_rows = fitted.reshape(2, local_vir * active, local_fit)
    change = all_passes(fit_rows, flat, give, eps_vir, row, act, n_vir)
    out = epilogue(eps_vir, row, flat, change.reshape(CHUNKS * n_fit, own * active, lanes))
    out = out.reshape(local_vir, active // 2, 2, lanes).transpose(0, 2, 1, 3)
    return out.reshape(local_vir, 2, active * pairs).transpose(1, 0, 2)


def choose(mesh):
    def body(*args):
        n_fit, n_vir = mesh.shape["fit"], mesh.shape["vir"]
        fitted, vcouple, actfock, eps_vir, eps_act, pair_energy, source = args
        local_vir, active, local_fit = fitted.shape[1:]
        fits = (
            n_fit == 4
            and CHUNKS == 3
            and n_vir == 8
            and n_vir % 2 == 0
            and 2 * pair_energy.shape[0] == 128
            and n_vir * 16 == 128
            and local_vir % (CHUNKS * n_fit * 5) == 0
            and vcouple.shape[1] % local_vir == 0
            and active % 8 == 0
            and local_fit % 128 == 0
        )
        return per_device(*args) if fits else plain_device(*args)

    return body


def solution(mesh):
    return jax.shard_map(
        choose(mesh),
        mesh=mesh,
        in_specs=(
            P(None, "vir", None, "fit"),
            P(None, "fit", None),
            P(),
            P("vir"),
            P(),
            P(),
            P(None, "vir", None),
        ),
        out_specs=P(None, "vir", None),
        check_vma=False,
    )
```
